256 devices in a mesh: band: 8 (over z), gy: 32 (over x, y, core).
Axes of the slice: x: 4, y: 4, z: 8, core: 2. Of those that a mesh axis runs over, the one named last changes fastest.
Arguments:
- orbitals: float32 [32, 32, 512, 256], P('band', None, 'gy'), may hold values from -11 to 11
- potentials: float32 [2, 32, 512, 256], P(None, None, 'gy'), may hold values from -1 to 3
- local_potential: float32 [32, 512, 256], P(None, 'gy'), may hold values from 0 to 1
- shifts: float32 [32], P('band'), may hold values from 0.05 to 0.8
Outputs:
- field_response: float32 [2, 32, 256, 512], P(None, 'band', 'gy')
The draws below stay inside these ranges and needn't reach their ends.
All inputs are finite; a program needn't handle non-finite values.
Results may differ from the reference program's by a relative error of at most 0.0003.
Values sent between devices are 32-bit elements; how exact they have to be, the bound alone decides.
A program may use at most 128 MiB of HBM per device.

```python
import math
import jax
import jax.numpy as jnp
from jax import lax

NX = 256
NY = 512
NZ = 32
NPOT = 2
SWEEPS = 3
NORB = 32


def draw_orbitals(key, part):
    rows = jnp.arange(NY, dtype=jnp.float32) / (NY - 1)
    values = jax.random.truncated_normal(key, -6.0, 6.0, (NORB, NZ, NY, NX), jnp.float32)
    envelope = jnp.sqrt(1.0 + 2.0 * rows)
    return values * envelope[None, None, :, None]


def draw_potentials(key, part):
    values = 1.0 + 0.5 * jax.random.truncated_normal(key, -4.0, 4.0, (NPOT, NZ, NY, NX), jnp.float32)
    return values


def steps_of(own_key, dims, cuts, least, top_value):
    def one(position, parts):
        heights = jax.random.uniform(jax.random.fold_in(jax.random.fold_in(own_key, 6), position), (parts,), jnp.float32, least / len(cuts), top_value / len(cuts))
        return jnp.repeat(jnp.exp(heights), dims[position] // parts).reshape((-1,) + (1,) * (len(dims) - position - 1))

    level = one(*cuts[0])
    for cut in cuts[1:]:
        level = level * one(*cut)
    return level


def setup_inputs(seed: int = 0) -> dict:
    keys = jax.random.split(jax.random.key(seed), 5)
    return {
        "orbitals": draw_orbitals(jax.random.fold_in(keys[4], 71), 0),
        "potentials": draw_potentials(jax.random.fold_in(keys[4], 71), 0),
        "local_potential": jnp.clip(1.0 * jax.random.uniform(keys[2], (NZ, NY, NX), jnp.float32) ** steps_of(keys[2], (NZ, NY, NX), ((1, 32),), -0.2, 0.2), 0.0, 1.0),
        "shifts": jnp.clip(jnp.exp(math.log(0.8) - 2.7725887 * jax.random.uniform(keys[3], (NORB,), jnp.float32) ** steps_of(keys[3], (NORB,), ((0, 8),), -0.2, 0.2)), 0.05, 0.8),
    }


spread_half = 3.5
screening = 0.25

def sine_table(length):
    index = jnp.arange(1, length + 1, dtype=jnp.int32)
    phase = index[:, None] * index[None, :] % (2 * (length + 1))
    scale = jnp.sqrt(jnp.float32(2.0) / (length + 1))
    return scale * jnp.sin(jnp.float32(jnp.pi) * phase.astype(jnp.float32) / (length + 1))

def coulomb(z_index, x_index, y_index):
    wave_z = jnp.pi * (z_index.astype(jnp.float32) + 1.0) / (NZ + 1)
    wave_x = jnp.pi * (x_index.astype(jnp.float32) + 1.0) / (NX + 1)
    wave_y = jnp.pi * (y_index.astype(jnp.float32) + 1.0) / (NY + 1)
    total = wave_z[:, None, None] * wave_z[:, None, None] + wave_x[None, :, None] * wave_x[None, :, None]
    total = total + wave_y[None, None, :] * wave_y[None, None, :] + screening
    return jnp.sqrt(4.0 * jnp.pi / total)

def beside(field, axis):
    size = field.shape[axis]
    upper = lax.slice_in_dim(field, 1, size, axis=axis)
    lower = lax.slice_in_dim(field, 0, size - 1, axis=axis)
    pad_upper = tuple(((0, 1) if i == axis else (0, 0) for i in range(field.ndim)))
    pad_lower = tuple(((1, 0) if i == axis else (0, 0) for i in range(field.ndim)))
    return jnp.pad(upper, pad_upper) + jnp.pad(lower, pad_lower)

def pad_rows(field):
    return jnp.pad(field, tuple(((1, 1) if i == field.ndim - 2 else (0, 0) for i in range(field.ndim))))

def operate(padded, local_potential, shift):
    center = padded[..., 1:-1, :]
    near = padded[..., 2:, :] + padded[..., :-2, :]
    near = near + beside(center, center.ndim - 1) + beside(center, center.ndim - 3)
    return (3.0 + local_potential + shift) * center - 0.5 * near

def chebyshev(source, apply_fn, shift):
    center_value = shift + spread_half
    ratio_start = center_value / spread_half
    weight_now = 1.0 / ratio_start
    direction = source / center_value
    residual = source
    iterate = jnp.zeros_like(source)
    for sweep in range(SWEEPS):
        iterate = iterate + direction
        residual = residual - apply_fn(direction)
        weight_next = 1.0 / (2.0 * ratio_start - weight_now)
        direction = weight_next * weight_now * direction + 2.0 * weight_next / spread_half * residual
        weight_now = weight_next
    return iterate + direction

def reference(orbitals, potentials, local_potential, shifts):

    def one_orbital(density, item):
        orbital, shift = item
        squares = orbital * orbital
        coefficient = lax.optimization_barrier(jnp.sum(potentials * squares[None], axis=(1, 2, 3))) / jnp.sum(squares)
        source = (potentials - coefficient[:, None, None, None]) * orbital[None]

        def apply_fn(field):
            return operate(pad_rows(field), local_potential, shift)
        response = chebyshev(source, apply_fn, shift)
        return (density - 4.0 * orbital[None] * response, None)
    density = lax.scan(one_orbital, jnp.zeros(potentials.shape, jnp.float32), (orbitals, shifts))[0]
    highest = lax.Precision.HIGHEST
    along_z = jnp.einsum('kz,pzyx->pkyx', sine_table(NZ), density, precision=highest)
    along_x = jnp.einsum('jx,pkyx->pkyj', sine_table(NX), along_z, precision=highest)
    along_y = jnp.einsum('my,pkyj->pkjm', sine_table(NY), along_x, precision=highest)
    weight = coulomb(jnp.arange(NZ, dtype=jnp.int32), jnp.arange(NX, dtype=jnp.int32), jnp.arange(NY, dtype=jnp.int32))
    return along_y * weight[None]
```

```python
import functools

import jax
import jax.numpy as jnp
import numpy as np
from jax import lax
from jax.experimental import pallas as pl
from jax.experimental.pallas import tpu as pltpu
from jax.sharding import PartitionSpec as P

NX, NY, NZ, NPOT, SWEEPS, NORB = 256, 512, 32, 2, 3, 32
NB, NG = 8, 32
NL = NORB // NB
NR = NY // NG
NF = NL * NPOT
H = 3
KZ, KX = NZ // NB, NX // NG
PK = NPOT * KZ
T = 128
ZO = 8
BLK = 4
NBLK = NR // BLK
HALO = NL * H + NPOT * H + 2
SPREAD, SCREEN = 3.5, 0.25
MESH = pl.DeviceIdType.MESH
f32, bf16 = jnp.float32, jnp.bfloat16


def sine(length):
    k = np.arange(1, length + 1, dtype=np.float64)
    return np.sqrt(2.0 / (length + 1)) * np.sin(np.pi * np.outer(k, k) / (length + 1))


def halves(table):
    high = table.astype(np.float32).astype(bf16)
    low = (table - high.astype(np.float64)).astype(np.float32).astype(bf16)
    return high, low


def tables():
    zh, zl = halves(sine(NZ))
    lz = np.zeros((NB, NPOT, KZ, NPOT, 3, NZ), bf16)
    for p in range(NPOT):
        for i, part in enumerate((zh, zh, zl)):
            lz[:, p, :, p, i, :] = part.reshape(NB, KZ, NZ)
    lz = lz.reshape(NB * PK, NPOT * 3 * NZ)
    sx = np.stack(halves(sine(NX)))
    sy = np.stack(halves(sine(NY)))
    st, y, j = np.meshgrid(np.arange(NG // 8), np.arange(NR), np.arange(8), indexing="ij")
    sy = sy[:, (NR * (8 * st + j) + y).reshape(-1), :]
    return lz, sx, sy


def split(value):
    high = value.astype(bf16)
    return high, (value - high.astype(f32)).astype(bf16)


def polynomial(shift):
    c = shift + SPREAD
    ratio = c / SPREAD
    now = 1.0 / ratio
    d, r, x = [1.0 / c], [jnp.ones_like(c)], []

    def add(a, b):
        out = []
        for i in range(max(len(a), len(b))):
            if i < len(a) and i < len(b):
                out.append(a[i] + b[i])
            else:
                out.append(a[i] if i < len(a) else b[i])
        return out

    for _ in range(SWEEPS):
        x = add(x, d)
        ad = [c * d[0]]
        for i in range(1, len(d)):
            ad.append(c * d[i] - 0.5 * d[i - 1])
        ad.append(-0.5 * d[-1])
        r = add(r, [-v for v in ad])
        after = 1.0 / (2.0 * ratio - now)
        d = add([after * now * v for v in d], [(2.0 * after / SPREAD) * v for v in r])
        now = after
    return add(x, d)


def kernel(
    orb_hbm, pot_hbm, loc_hbm, shift_ref, lz_hbm, sx_hbm, sy_hbm, out_ref,
    orbv, potv, locv, lz, sx, sy, hs, hr, f0, f1, f2, wv, cf, pc, msg, rmsg,
    part, rbf, rbb, ov, rv, qv, wgt,
    load_sem, hsend, hrecv, msend, mrecv, fsend, frecv, bsend, brecv, asend, arecv,
):
    band, gy = lax.axis_index("band"), lax.axis_index("gy")

    barrier = pltpu.get_barrier_semaphore()

    def greet(d, carry):
        pl.semaphore_signal(barrier, 1, device_id=(band, lax.rem(gy + d, NG)), device_id_type=MESH)
        return carry

    lax.fori_loop(1, NG, greet, 0)
    for d in (1, NB - 1):
        pl.semaphore_signal(barrier, 1, device_id=(lax.rem(band + d, NB), gy), device_id_type=MESH)

    loads = []
    for x in range(2):
        for src, dst in ((orb_hbm, orbv), (pot_hbm, potv), (loc_hbm, locv)):
            loads.append(pltpu.make_async_copy(src.at[:, pl.ds(T * x, T)], dst.at[x], load_sem.at[len(loads)]))
    for src, dst in ((lz_hbm, lz), (sx_hbm, sx), (sy_hbm, sy)):
        loads.append(pltpu.make_async_copy(src, dst, load_sem.at[len(loads)]))
    for copy in loads:
        copy.start()

    zero = jnp.zeros((8, T), f32)

    def clear(r, carry):
        for f in range(NF):
            for x in range(2):
                for field in (f0, f1, f2):
                    field[f, r, x, 0:8, :] = zero
                    field[f, r, x, ZO + NZ : ZO + NZ + 8, :] = zero
        return carry

    lax.fori_loop(0, NR + 2 * H, clear, 0)

    for n in range(NL):
        a = polynomial(jnp.full((8, T), shift_ref[n], f32))
        inverse = 1.0 / a[3]
        pc[n, 0] = a[2] * inverse
        pc[n, 1] = a[1] * inverse
        pc[n, 2] = a[0] * inverse
        pc[n, 3] = -4.0 * a[3]

    for copy in loads[:6]:
        copy.wait()

    def orb_row(n, x, y):
        return orbv[x, pl.ds(n * NZ * NR + y, NZ, stride=NR), :]

    def pot_row(p, x, y):
        return potv[x, pl.ds(p * NZ * NR + y, NZ, stride=NR), :]

    def loc_row(x, y):
        return locv[x, pl.ds(y, NZ, stride=NR), :]

    for side in range(2):
        for i in range(H):
            y = i if side == 0 else NR - H + i
            for x in range(2):
                for n in range(NL):
                    hs[side, n * H + i, x] = orb_row(n, x, y)
                for p in range(NPOT):
                    hs[side, NL * H + p * H + i, x] = pot_row(p, x, y)
        for i in range(2):
            y = i if side == 0 else NR - 2 + i
            for x in range(2):
                hs[side, NL * H + NPOT * H + i, x] = loc_row(x, y)

    def sums(i, acc):
        acc = list(acc)
        for x in range(2):
            pots = [potv[x, pl.ds(p * NZ * NR + i * 8, 8), :] for p in range(NPOT)]
            for n in range(NL):
                o = orbv[x, pl.ds(n * NZ * NR + i * 8, 8), :]
                q = o * o
                for p in range(NPOT):
                    acc[p * NL + n] = acc[p * NL + n] + pots[p] * q
                acc[NF + n] = acc[NF + n] + q
        return tuple(acc)

    acc = lax.fori_loop(0, NZ * NR // 8, sums, tuple(zero for _ in range(NF + NL)), unroll=4)
    lane1 = lax.broadcasted_iota(jnp.int32, (1, T), 1)
    row = jnp.zeros((1, T), f32)
    for i, a in enumerate(acc):
        total = jnp.sum(jnp.sum(a, axis=0, keepdims=True), axis=1, keepdims=True)
        row = jnp.where(lane1 == i, total, row)
    msg[...] = row

    pl.semaphore_wait(barrier, NG + 1)

    def tell(d, carry):
        pltpu.make_async_remote_copy(
            msg, rmsg.at[d], msend, mrecv,
            device_id=(band, lax.rem(gy + d, NG)), device_id_type=MESH,
        ).start()
        return carry

    lax.fori_loop(1, NG, tell, 0)
    halo = []
    for side in range(2):
        target = lax.rem(gy + (NG - 1 if side == 0 else 1), NG)
        copy = pltpu.make_async_remote_copy(
            hs.at[side], hr.at[1 - side], hsend.at[side], hrecv.at[1 - side],
            device_id=(band, target), device_id_type=MESH,
        )
        copy.start()
        halo.append(copy)

    def index_of(shape, axis):
        return lax.broadcasted_iota(jnp.int32, shape, axis)

    shape = (PK * KX, NY)
    r_index = index_of(shape, 0)
    kz = band * KZ + lax.rem(lax.div(r_index, KX), KZ)
    kx = gy * KX + lax.rem(r_index, KX)
    qz = jnp.pi * (kz.astype(f32) + 1.0) / (NZ + 1)
    qx = jnp.pi * (kx.astype(f32) + 1.0) / (NX + 1)
    qy = jnp.pi * (index_of(shape, 1).astype(f32) + 1.0) / (NY + 1)
    wgt[...] = jnp.sqrt(4.0 * jnp.pi / (qz * qz + qx * qx + qy * qy + SCREEN))

    def own_w(y, carry):
        for x in range(2):
            wv[y + H, x] = 1.0 - 2.0 * loc_row(x, y)
        return carry

    lax.fori_loop(0, NR, own_w, 0)

    pltpu.make_async_copy(rmsg.at[pl.ds(0, NG - 1)], rmsg.at[pl.ds(0, NG - 1)], mrecv).wait()
    total = msg[...]
    for d in range(1, NG):
        total = total + rmsg[d]
    for n in range(NL):
        norm = total[:, NF + n : NF + n + 1]
        for p in range(NPOT):
            value = total[:, p * NL + n : p * NL + n + 1] / norm
            cf[n * NPOT + p] = jnp.broadcast_to(value, (8, T))

    def whole(tile):
        return jnp.concatenate([tile] * (NZ // 8), axis=0)

    inner = pl.ds(ZO, NZ)

    def own_source(y, carry):
        for x in range(2):
            pots = [pot_row(p, x, y) for p in range(NPOT)]
            for n in range(NL):
                o = orb_row(n, x, y)
                for p in range(NPOT):
                    f = n * NPOT + p
                    f0[f, y + H, x, inner, :] = (pots[p] - whole(cf[f])) * o
        return carry

    lax.fori_loop(0, NR, own_source, 0)

    lane = lax.broadcasted_iota(jnp.int32, (NZ, T), 1)
    first, last = lane == 0, lane == T - 1
    nought = jnp.zeros((NZ, T), f32)

    def near(field, f, r):
        c = [field[f, r, x, inner, :] for x in range(2)]
        up = [pltpu.roll(v, 1, 1) for v in c]
        down = [pltpu.roll(v, T - 1, 1) for v in c]
        beside = [
            jnp.where(first, nought, up[0]) + jnp.where(last, down[1], down[0]),
            jnp.where(first, up[0], up[1]) + jnp.where(last, nought, down[1]),
        ]
        sums = []
        for x in range(2):
            z = field[f, r, x, pl.ds(ZO - 1, NZ), :] + field[f, r, x, pl.ds(ZO + 1, NZ), :]
            y = field[f, r - 1, x, inner, :] + field[f, r + 1, x, inner, :]
            sums.append(beside[x] + (z + y))
        return c, sums

    def sweep_one(r, mask=None):
        for n in range(NL):
            ws = [wv[r, x] + whole(pc[n, 0]) for x in range(2)]
            for p in range(NPOT):
                f = n * NPOT + p
                c, s = near(f0, f, r)
                for x in range(2):
                    value = s[x] + ws[x] * c[x]
                    f1[f, r, x, inner, :] = value if mask is None else value * mask

    def sweep_two(r, mask=None):
        for n in range(NL):
            beta = whole(pc[n, 1])
            for p in range(NPOT):
                f = n * NPOT + p
                c, s = near(f1, f, r)
                for x in range(2):
                    value = s[x] + wv[r, x] * c[x] + beta * f0[f, r, x, inner, :]
                    f2[f, r, x, inner, :] = value if mask is None else value * mask

    def loop(low, high, body):
        def step(r, carry):
            body(r)
            return carry

        lax.fori_loop(low, high, step, 0)

    loop(H + 1, H + NR - 1, sweep_one)
    loop(H + 2, H + NR - 2, sweep_two)

    low_mask = jnp.where(gy == 0, 0.0, 1.0).astype(f32)
    high_mask = jnp.where(gy == NG - 1, 0.0, 1.0).astype(f32)
    masks = (low_mask, high_mask)
    for side in range(2):
        halo[side].wait_recv()
    for side in range(2):
        for i in range(H):
            r = i if side == 0 else H + NR + i
            for x in range(2):
                for n in range(NL):
                    o = hr[side, n * H + i, x] * masks[side]
                    for p in range(NPOT):
                        f = n * NPOT + p
                        f0[f, r, x, inner, :] = (hr[side, NL * H + p * H + i, x] - whole(cf[f])) * o
        for i in range(2):
            r = 1 + i if side == 0 else H + NR + i
            for x in range(2):
                wv[r, x] = 1.0 - 2.0 * hr[side, NL * H + NPOT * H + i, x]
    loop(1, H, lambda r: sweep_one(r, low_mask))
    loop(H, H + 1, sweep_one)
    loop(H + NR - 1, H + NR, sweep_one)
    loop(H + NR, H + NR + 2, lambda r: sweep_one(r, high_mask))
    loop(H - 1, H, lambda r: sweep_two(r, low_mask))
    loop(H, H + 2, sweep_two)
    loop(H + NR - 2, H + NR, sweep_two)
    loop(H + NR, H + NR + 1, lambda r: sweep_two(r, high_mask))

    loads[6].wait()

    def last_sweep(y):
        r = y + H
        density = [[None, None] for _ in range(NPOT)]
        for n in range(NL):
            beta, gamma = whole(pc[n, 2]), whole(pc[n, 3])
            orbs = [orb_row(n, x, y) * gamma for x in range(2)]
            for p in range(NPOT):
                f = n * NPOT + p
                c, s = near(f2, f, r)
                for x in range(2):
                    value = s[x] + wv[r, x] * c[x] + beta * f0[f, r, x, inner, :]
                    term = orbs[x] * value
                    old = density[p][x]
                    density[p][x] = term if old is None else old + term
        for x in range(2):
            stack = []
            for p in range(NPOT):
                high, low = split(density[p][x])
                stack += [high, low, high]
            along_z = jnp.dot(lz[...], jnp.concatenate(stack, axis=0), preferred_element_type=f32)
            for b in range(NB):
                part[b, y, :, T * x : T * (x + 1)] = along_z[b * PK : (b + 1) * PK, :]

    ahead, behind = lax.rem(band + 1, NB), lax.rem(band + NB - 1, NB)

    def forward(step, k):
        rows = pl.ds(k * BLK, BLK)
        chunk = lax.rem(band + (5 - step), NB)
        return pltpu.make_async_remote_copy(
            part.at[chunk, rows], rbf.at[step - 1, rows], fsend.at[step - 1, k], frecv.at[step - 1, k],
            device_id=(ahead, gy), device_id_type=MESH,
        )

    def backward(step, k):
        rows = pl.ds(k * BLK, BLK)
        chunk = lax.rem(band + (NB - 5 + step), NB)
        return pltpu.make_async_remote_copy(
            part.at[chunk, rows], rbb.at[step - 1, rows], bsend.at[step - 1, k], brecv.at[step - 1, k],
            device_id=(behind, gy), device_id_type=MESH,
        )

    def goes_forward(step, k):
        return step > 1 or k < NBLK // 2

    def goes_backward(step, k):
        return step > 1 or k >= NBLK // 2

    def reduce_step(step, k):
        rows = pl.ds(k * BLK, BLK)
        if goes_forward(step, k):
            if step > 1 and goes_forward(step - 1, k):
                forward(step - 1, k).wait_recv()
                chunk = lax.rem(band + (5 - step), NB)
                part[chunk, rows] = part[chunk, rows] + rbf[step - 2, rows]
            forward(step, k).start()
        if goes_backward(step, k):
            if step > 1 and goes_backward(step - 1, k):
                backward(step - 1, k).wait_recv()
                chunk = lax.rem(band + (NB - 5 + step), NB)
                part[chunk, rows] = part[chunk, rows] + rbb[step - 2, rows]
            backward(step, k).start()

    for k in range(NBLK):
        loop(k * BLK, (k + 1) * BLK, last_sweep)
        reduce_step(1, k)
    for step in range(2, 5):
        for k in range(NBLK):
            reduce_step(step, k)

    loads[7].wait()
    sums_of = []
    for k in range(NBLK):
        rows = pl.ds(k * BLK, BLK)
        forward(4, k).wait_recv()
        backward(4, k).wait_recv()
        sums_of.append((part[band, rows] + (rbf[3, rows] + rbb[3, rows])).reshape(BLK * PK, NX))
    high, low = split(jnp.concatenate(sums_of, axis=0))

    def by_rows(a, b):
        return lax.dot_general(a, b, (((1,), (1,)), ((), ())), preferred_element_type=f32)

    along_x = by_rows(sx[0], high) + by_rows(sx[0], low) + by_rows(sx[1], high)
    ov[...] = along_x.reshape(NG, KX, NR * PK)

    def scatter(d, carry):
        target = lax.rem(gy + d, NG)
        pltpu.make_async_remote_copy(
            ov.at[target], rv.at[gy], asend, arecv, device_id=(band, target), device_id_type=MESH
        ).start()
        return carry

    lax.fori_loop(1, NG, scatter, 0)
    rv[gy] = ov[gy]
    loads[8].wait()

    others = pl.ds(0, NG - 1)
    pltpu.make_async_copy(rv.at[others], rv.at[others], arecv).wait()

    lane8 = lax.rem(lax.broadcasted_iota(jnp.int32, (KX, T), 1), 8)
    for st in range(NG // 8):
        tiles = [rv[st * 8 + j] for j in range(8)]
        for pk in range(PK):
            got = None
            for j in range(8):
                shift = (j - pk) % T
                moved = tiles[j] if shift == 0 else pltpu.roll(tiles[j], shift, 1)
                got = moved if got is None else jnp.where(lane8 == j, moved, got)
            qv[pk * KX : (pk + 1) * KX, st * T : (st + 1) * T] = got
    high, low = split(qv[...])
    along_y = (
        jnp.dot(high, sy[0], preferred_element_type=f32)
        + jnp.dot(low, sy[0], preferred_element_type=f32)
        + jnp.dot(high, sy[1], preferred_element_type=f32)
    )
    out_ref[...] = along_y * wgt[...]

    for copy in halo:
        copy.wait_send()
    pltpu.make_async_copy(rmsg.at[pl.ds(0, NG - 1)], rmsg.at[pl.ds(0, NG - 1)], msend).wait()
    for step in range(1, 5):
        for k in range(NBLK):
            if goes_forward(step, k):
                forward(step, k).wait_send()
            if goes_backward(step, k):
                backward(step, k).wait_send()
    pltpu.make_async_copy(rv.at[others], rv.at[others], asend).wait()


def per_device(orbitals, potentials, local_potential, shifts):
    lz, sx, sy = tables()
    anywhere = pl.BlockSpec(memory_space=pl.ANY)
    rows = NR + 2 * H
    field = pltpu.VMEM((NF, rows, 2, NZ + 16, T), f32)
    dma = pltpu.SemaphoreType.DMA
    out = pl.pallas_call(
        kernel,
        out_shape=jax.ShapeDtypeStruct((PK * KX, NY), f32),
        in_specs=[anywhere, anywhere, anywhere, pl.BlockSpec(memory_space=pltpu.SMEM)] + [anywhere] * 3,
        out_specs=pl.BlockSpec(memory_space=pltpu.VMEM),
        scratch_shapes=[
            pltpu.VMEM((2, NL * NZ * NR, T), f32),
            pltpu.VMEM((2, NPOT * NZ * NR, T), f32),
            pltpu.VMEM((2, NZ * NR, T), f32),
            pltpu.VMEM((NB * PK, NPOT * 3 * NZ), bf16),
            pltpu.VMEM((2, NX, NX), bf16),
            pltpu.VMEM((2, NY, NY), bf16),
            pltpu.VMEM((2, HALO, 2, NZ, T), f32),
            pltpu.VMEM((2, HALO, 2, NZ, T), f32),
            field,
            field,
            field,
            pltpu.VMEM((rows, 2, NZ, T), f32),
            pltpu.VMEM((NF, 8, T), f32),
            pltpu.VMEM((NL, 4, 8, T), f32),
            pltpu.VMEM((1, T), f32),
            pltpu.VMEM((NG, 1, T), f32),
            pltpu.VMEM((NB, NR, PK, NX), f32),
            pltpu.VMEM((4, NR, PK, NX), f32),
            pltpu.VMEM((4, NR, PK, NX), f32),
            pltpu.VMEM((NG, KX, NR * PK), f32),
            pltpu.VMEM((NG, KX, NR * PK), f32),
            pltpu.VMEM((PK * KX, NG * NR), f32),
            pltpu.VMEM((PK * KX, NY), f32),
            dma((9,)),
            dma((2,)),
            dma((2,)),
            dma,
            dma,
            dma((4, NBLK)),
            dma((4, NBLK)),
            dma((4, NBLK)),
            dma((4, NBLK)),
            dma,
            dma,
        ],
        compiler_params=pltpu.CompilerParams(
            collective_id=0, has_side_effects=True, vmem_limit_bytes=56 * 1024 * 1024
        ),
    )(
        orbitals.reshape(NL * NZ * NR, NX),
        potentials.reshape(NPOT * NZ * NR, NX),
        local_potential.reshape(NZ * NR, NX),
        shifts,
        jnp.asarray(lz),
        jnp.asarray(sx),
        jnp.asarray(sy),
    )
    return out.reshape(NPOT, KZ, KX, NY)


def solution(mesh):
    placed = (
        P("band", None, "gy", None),
        P(None, None, "gy", None),
        P(None, "gy", None),
        P("band"),
    )
    return jax.shard_map(
        per_device,
        mesh=mesh,
        in_specs=placed,
        out_specs=P(None, "band", "gy", None),
        check_vma=False,
    )
```

```python
import jax
import jax.numpy as jnp
import numpy as np
from jax import lax
from jax.experimental import pallas as pl
from jax.experimental.pallas import tpu as pltpu
from jax.sharding import PartitionSpec as P

NX, NY, NZ, NPOT, SWEEPS, NORB = 256, 512, 32, 2, 3, 32
NB, NG = 8, 32
NL = NORB // NB
NR = NY // NG
NF = NL * NPOT
H = 3
KZ, KX = NZ // NB, NX // NG
PK = NPOT * KZ
T = 128
ZO = 8
ROWS = NR + 2 * H
ZB = ZO + NZ
SLAB = ROWS * 2 * ZB + ZO
PIECES = ((3, 3), (6, 3), (9, 4), (13, 3), (0, 3))
GROUP = 4
SPREAD, SCREEN = 3.5, 0.25
MESH = pl.DeviceIdType.MESH
f32, bf16 = jnp.float32, jnp.bfloat16


def sine(length):
    k = np.arange(1, length + 1, dtype=np.float64)
    return np.sqrt(2.0 / (length + 1)) * np.sin(np.pi * np.outer(k, k) / (length + 1))


def halves(table):
    high = table.astype(np.float32).astype(bf16)
    low = (table - high.astype(np.float64)).astype(np.float32).astype(bf16)
    return high, low


def tables():
    zh, zl = halves(sine(NZ))
    lz = np.zeros((NB, NPOT, KZ, NPOT, 3, NZ), bf16)
    for p in range(NPOT):
        for i, part in enumerate((zh, zh, zl)):
            lz[:, p, :, p, i, :] = part.reshape(NB, KZ, NZ)
    lz = lz.reshape(NB * PK, NPOT * 3 * NZ)
    sx = np.stack(halves(sine(NX)))
    sy = np.stack(halves(sine(NY)))
    st, y, j = np.meshgrid(np.arange(NG // 8), np.arange(NR), np.arange(8), indexing="ij")
    sy = sy[:, (NR * (8 * st + j) + y).reshape(-1), :]
    return lz, sx, sy


def split(value):
    high = value.astype(bf16)
    return high, (value - high.astype(f32)).astype(bf16)


def polynomial(shift):
    c = shift + SPREAD
    ratio = c / SPREAD
    now = 1.0 / ratio
    d, r, x = [1.0 / c], [jnp.ones_like(c)], []

    def add(a, b):
        out = []
        for i in range(max(len(a), len(b))):
            if i < len(a) and i < len(b):
                out.append(a[i] + b[i])
            else:
                out.append(a[i] if i < len(a) else b[i])
        return out

    for _ in range(SWEEPS):
        x = add(x, d)
        ad = [c * d[0]]
        for i in range(1, len(d)):
            ad.append(c * d[i] - 0.5 * d[i - 1])
        ad.append(-0.5 * d[-1])
        r = add(r, [-v for v in ad])
        after = 1.0 / (2.0 * ratio - now)
        d = add([after * now * v for v in d], [(2.0 * after / SPREAD) * v for v in r])
        now = after
    return add(x, d)


def kernel(
    orb_hbm, pot_hbm, loc_hbm, shift_ref, lz_hbm, sx_hbm, sy_hbm, out_ref,
    orbv, potv, locv, lz, sx, sy, f0, f1, f2, cf, pc, msg, rmsg,
    e0, e1, part, inbox, dv, ov, rv, wgt,
    load_sem, table_sem, hsend, hrecv, msend, mrecv, rsend, rrecv, asend, arecv,
):
    band, gy = lax.axis_index("band"), lax.axis_index("gy")

    barrier = pltpu.get_barrier_semaphore()
    for d in range(1, NG):
        pl.semaphore_signal(barrier, 1, device_id=(band, lax.rem(gy + d, NG)), device_id_type=MESH)
    for d in range(1, NB):
        pl.semaphore_signal(barrier, 1, device_id=(lax.rem(band + d, NB), gy), device_id_type=MESH)

    arrays = ((orb_hbm, orbv), (pot_hbm, potv), (loc_hbm, locv))
    for y in range(NR):
        for i, (src, dst) in enumerate(arrays):
            pltpu.make_async_copy(src.at[:, y], dst.at[H + y], load_sem.at[i, y // GROUP]).start()
    tables_in = []
    for i, (src, dst) in enumerate(((lz_hbm, lz), (sx_hbm, sx), (sy_hbm, sy))):
        tables_in.append(pltpu.make_async_copy(src, dst, table_sem.at[i]))
        tables_in[-1].start()

    zero = jnp.zeros((8, T), f32)

    def sums(r, acc):
        acc = list(acc)
        for z in range(NZ // 8):
            for x in range(2):
                cols = slice(T * x, T * (x + 1))
                pots = [potv[r, p * NZ + z * 8 : p * NZ + z * 8 + 8, cols] for p in range(NPOT)]
                for n in range(NL):
                    o = orbv[r, n * NZ + z * 8 : n * NZ + z * 8 + 8, cols]
                    q = o * o
                    for p in range(NPOT):
                        acc[p * NL + n] = acc[p * NL + n] + pots[p] * q
                    acc[NF + n] = acc[NF + n] + q
        return tuple(acc)

    acc = tuple(zero for _ in range(NF + NL))
    for g in range(NR // GROUP):
        rows = pl.ds(H + g * GROUP, GROUP)
        for i, (_, dst) in enumerate(arrays):
            pltpu.make_async_copy(dst.at[rows], dst.at[rows], load_sem.at[i, g]).wait()
        acc = lax.fori_loop(H + g * GROUP, H + (g + 1) * GROUP, sums, acc)
    lane1 = lax.broadcasted_iota(jnp.int32, (1, T), 1)
    row = jnp.zeros((1, T), f32)
    for i, a in enumerate(acc):
        total = jnp.sum(jnp.sum(a, axis=0, keepdims=True), axis=1, keepdims=True)
        row = jnp.where(lane1 == i, total, row)
    msg[...] = row

    pl.semaphore_wait(barrier, NG - 1 + NB - 1)

    for d in range(1, NG):
        pltpu.make_async_remote_copy(
            msg, rmsg.at[d], msend, mrecv,
            device_id=(band, lax.rem(gy + d, NG)), device_id_type=MESH,
        ).start()

    halo = []
    for side in range(2):
        target = lax.rem(gy + (NG - 1 if side == 0 else 1), NG)
        for i, (_, dst) in enumerate(arrays):
            width = H if i < 2 else H - 1
            if side == 0:
                src, to = pl.ds(H, width), pl.ds(H + NR, width)
            else:
                src, to = pl.ds(H + NR - width, width), pl.ds(H - width, width)
            copy = pltpu.make_async_remote_copy(
                dst.at[src], dst.at[to], hsend.at[side, i], hrecv.at[side, i],
                device_id=(band, target), device_id_type=MESH,
            )
            copy.start()
            halo.append(copy)

    def clear(i, carry):
        for f in range(NF):
            for field in (f0, f1, f2):
                field[f, pl.ds(pl.multiple_of(i * ZB, 8), ZO), :] = zero
        for n in range(NL):
            e0[n, pl.ds(pl.multiple_of(i * ZB, 8), ZO), :] = zero
        return carry

    lax.fori_loop(0, 2 * ROWS + 1, clear, 0)

    for n in range(NL):
        a = polynomial(jnp.full((8, T), shift_ref[n], f32))
        inverse = 1.0 / a[3]
        pc[n, 0] = a[2] * inverse
        pc[n, 1] = a[1] * inverse
        pc[n, 2] = a[0] * inverse
        pc[n, 3] = -4.0 * a[3]

    def index_of(shape, axis):
        return lax.broadcasted_iota(jnp.int32, shape, axis)

    shape = (PK * KX, NY)
    r_index = index_of(shape, 0)
    kz = band * KZ + lax.rem(lax.div(r_index, KX), KZ)
    kx = gy * KX + lax.rem(r_index, KX)
    qz = jnp.pi * (kz.astype(f32) + 1.0) / (NZ + 1)
    qx = jnp.pi * (kx.astype(f32) + 1.0) / (NX + 1)
    qy = jnp.pi * (index_of(shape, 1).astype(f32) + 1.0) / (NY + 1)
    wgt[...] = jnp.sqrt(4.0 * jnp.pi / (qz * qz + qx * qx + qy * qy + SCREEN))

    def whole(tile):
        return jnp.concatenate([tile] * (NZ // 8), axis=0)

    def at(r, x, shift=0):
        return pl.ds(pl.multiple_of((r * 2 + x) * ZB + ZO, 8) + shift, NZ)

    def half(ref, r, i, x):
        return ref[r, i * NZ : (i + 1) * NZ, x * T : (x + 1) * T]

    def w_of(r, x):
        return 1.0 - 2.0 * half(locv, r, 0, x)

    def source(r, mask=None):
        for x in range(2):
            pots = [half(potv, r, p, x) for p in range(NPOT)]
            for n in range(NL):
                o = half(orbv, r, n, x)
                if mask is not None:
                    o = o * mask
                for p in range(NPOT):
                    f = n * NPOT + p
                    f0[f, at(r, x), :] = (pots[p] - whole(cf[f])) * o

    lane = lax.broadcasted_iota(jnp.int32, (NZ, T), 1)
    first, last = lane == 0, lane == T - 1
    nought = jnp.zeros((NZ, T), f32)

    def near(field, f, r):
        c = [field[f, at(r, x), :] for x in range(2)]
        up = [pltpu.roll(v, 1, 1) for v in c]
        down = [pltpu.roll(v, T - 1, 1) for v in c]
        beside = [
            jnp.where(first, nought, up[0]) + jnp.where(last, down[1], down[0]),
            jnp.where(first, up[0], up[1]) + jnp.where(last, nought, down[1]),
        ]
        found = []
        for x in range(2):
            z = field[f, at(r, x, -1), :] + field[f, at(r, x, 1), :]
            y = field[f, at(r - 1, x), :] + field[f, at(r + 1, x), :]
            found.append(beside[x] + (z + y))
        return c, found

    def sweep_one(r, mask=None):
        w = [w_of(r, x) for x in range(2)]
        for n in range(NL):
            ws = [w[x] + whole(pc[n, 0]) for x in range(2)]
            for p in range(NPOT):
                f = n * NPOT + p
                c, s = near(f0, f, r)
                for x in range(2):
                    value = s[x] + ws[x] * c[x]
                    f1[f, at(r, x), :] = value if mask is None else value * mask

    def products(r):
        for x in range(2):
            pots = [half(potv, r, p, x) for p in range(NPOT)]
            for n in range(NL):
                o = half(orbv, r, n, x)
                e0[n, at(r, x), :] = o
                for p in range(NPOT):
                    f0[n * NPOT + p, at(r, x), :] = pots[p] * o

    def sweep_products(r):
        w = [w_of(r, x) for x in range(2)]
        for n in range(NL):
            ws = [w[x] + whole(pc[n, 0]) for x in range(2)]
            for src, dst, f in ((f0, f1, n * NPOT), (f0, f1, n * NPOT + 1), (e0, e1, n)):
                c, s = near(src, f, r)
                for x in range(2):
                    dst[f, at(r, x), :] = s[x] + ws[x] * c[x]

    def settle_source(r):
        for x in range(2):
            for n in range(NL):
                o = e0[n, at(r, x), :]
                for p in range(NPOT):
                    f = n * NPOT + p
                    f0[f, at(r, x), :] = f0[f, at(r, x), :] - whole(cf[f]) * o

    def settle_first(r):
        for x in range(2):
            for n in range(NL):
                o = e1[n, at(r, x), :]
                for p in range(NPOT):
                    f = n * NPOT + p
                    f1[f, at(r, x), :] = f1[f, at(r, x), :] - whole(cf[f]) * o

    def sweep_two(r, mask=None):
        w = [w_of(r, x) for x in range(2)]
        for n in range(NL):
            beta = whole(pc[n, 1])
            for p in range(NPOT):
                f = n * NPOT + p
                c, s = near(f1, f, r)
                for x in range(2):
                    value = s[x] + w[x] * c[x] + beta * f0[f, at(r, x), :]
                    f2[f, at(r, x), :] = value if mask is None else value * mask

    def last_sweep(r):
        w = [w_of(r, x) for x in range(2)]
        density = [[None, None] for _ in range(NPOT)]
        for n in range(NL):
            beta, gamma = whole(pc[n, 2]), whole(pc[n, 3])
            orbs = [half(orbv, r, n, x) * gamma for x in range(2)]
            for p in range(NPOT):
                f = n * NPOT + p
                c, s = near(f2, f, r)
                for x in range(2):
                    value = s[x] + w[x] * c[x] + beta * f0[f, at(r, x), :]
                    term = orbs[x] * value
                    old = density[p][x]
                    density[p][x] = term if old is None else old + term
        for x in range(2):
            stack = []
            for p in range(NPOT):
                high, low = split(density[p][x])
                stack += [high, low, high]
            along_z = jnp.dot(lz[...], jnp.concatenate(stack, axis=0), preferred_element_type=f32)
            for b in range(NB):
                part[b, r - H, :, T * x : T * (x + 1)] = along_z[b * PK : (b + 1) * PK, :]

    def send(k, way, kind):
        low, count = PIECES[k]
        far, reach = ((4, 2), (3, 1), (1, 1), (2, 2))[kind]
        rows = part_rows(k, way) if kind == 0 else pl.ds(low, count)
        chunk = lax.rem(band + (far if way == 0 else NB - far), NB)
        to = lax.rem(band + (reach if way == 0 else NB - reach), NB)
        return pltpu.make_async_remote_copy(
            part.at[chunk, rows], inbox.at[way, kind, rows], rsend.at[way, kind, k], rrecv.at[way, kind, k],
            device_id=(to, gy), device_id_type=MESH,
        )

    def part_rows(k, way):
        low, count = PIECES[k]
        cut = (count + (k % 2)) // 2
        return pl.ds(low, cut) if way == 0 else pl.ds(low + cut, count - cut)

    def begin(k):
        for kind in (0, 1, 2):
            for way in range(2):
                send(k, way, kind).start()

    def middle(k):
        low, count = PIECES[k]
        rows = pl.ds(low, count)
        for way in range(2):
            send(k, way, 0).wait_recv()
            send(k, way, 1).wait_recv()
            chunk = lax.rem(band + (2 if way == 0 else NB - 2), NB)
            part[chunk, rows] = part[chunk, rows] + inbox[way, 1, rows]
            some = part_rows(k, way)
            part[chunk, some] = part[chunk, some] + inbox[way, 0, some]
            send(k, way, 3).start()

    def finish(k):
        low, count = PIECES[k]
        rows = pl.ds(low, count)
        for kind in (2, 3):
            for way in range(2):
                send(k, way, kind).wait_recv()
        value = part[band, rows] + ((inbox[0, 2, rows] + inbox[1, 2, rows]) + (inbox[0, 3, rows] + inbox[1, 3, rows]))
        dv[low * PK : (low + count) * PK, :] = value.reshape(count * PK, NX)

    def loop(low, high, body):
        def step(r, carry):
            body(r)
            return carry

        if high == low + 1:
            body(low)
        else:
            lax.fori_loop(low, high, step, 0)

    loop(H, H + NR, products)
    loop(H + 1, H + NR - 1, sweep_products)

    pltpu.make_async_copy(rmsg.at[pl.ds(0, NG - 1)], rmsg.at[pl.ds(0, NG - 1)], mrecv).wait()
    total = msg[...]
    for d in range(1, NG):
        total = total + rmsg[d]
    for n in range(NL):
        norm = total[:, NF + n : NF + n + 1]
        for p in range(NPOT):
            value = total[:, p * NL + n : p * NL + n + 1] / norm
            cf[n * NPOT + p] = jnp.broadcast_to(value, (8, T))

    done = [H, H + 1, H + 2, H + 3]
    for k in range(3):
        end = H + PIECES[k][0] + PIECES[k][1]
        for i, body in enumerate((settle_source, settle_first, sweep_two, last_sweep)):
            stop = min(end + 3 - i, H + NR - i)
            loop(done[i], stop, body)
            done[i] = stop
            if k == 0 and i == 2:
                tables_in[0].wait()
        begin(k)
        if k > 0:
            middle(k - 1)

    low_mask = jnp.where(gy == 0, 0.0, 1.0).astype(f32)
    high_mask = jnp.where(gy == NG - 1, 0.0, 1.0).astype(f32)
    for copy in halo:
        copy.wait_recv()
    top = H + NR
    loop(top, top + 3, lambda r: source(r, high_mask))
    loop(top - 1, top, sweep_one)
    loop(top, top + 2, lambda r: sweep_one(r, high_mask))
    loop(top - 2, top, sweep_two)
    loop(top, top + 1, lambda r: sweep_two(r, high_mask))
    loop(top - 3, top, last_sweep)
    begin(3)
    middle(2)
    loop(0, H, lambda r: source(r, low_mask))
    loop(1, H, lambda r: sweep_one(r, low_mask))
    loop(H, H + 1, sweep_one)
    loop(H - 1, H, lambda r: sweep_two(r, low_mask))
    loop(H, H + 2, sweep_two)
    loop(H, H + 3, last_sweep)
    begin(4)
    middle(3)
    finish(0)
    finish(1)
    finish(2)
    middle(4)
    finish(3)
    finish(4)

    tables_in[1].wait()
    high, low = split(dv[...])

    def by_rows(a, b):
        return lax.dot_general(a, b, (((1,), (1,)), ((), ())), preferred_element_type=f32)

    along_x = by_rows(sx[0], high) + by_rows(sx[0], low) + by_rows(sx[1], high)
    ov[...] = along_x.reshape(NG, KX, NR * PK)

    for d in range(1, NG):
        target = lax.rem(gy + d, NG)
        pltpu.make_async_remote_copy(
            ov.at[target], rv.at[gy], asend, arecv, device_id=(band, target), device_id_type=MESH
        ).start()
    rv[gy] = ov[gy]
    tables_in[2].wait()

    others = pl.ds(0, NG - 1)
    pltpu.make_async_copy(rv.at[others], rv.at[others], arecv).wait()

    lane8 = lax.rem(lax.broadcasted_iota(jnp.int32, (KX, T), 1), 8)
    along_y = None
    for pair in range(NG // 16):
        columns = []
        for st in (2 * pair, 2 * pair + 1):
            tiles = [rv[st * 8 + j] for j in range(8)]
            column = []
            for pk in range(PK):
                got = None
                for j in range(8):
                    shift = (j - pk) % T
                    moved = tiles[j] if shift == 0 else pltpu.roll(tiles[j], shift, 1)
                    got = moved if got is None else jnp.where(lane8 == j, moved, got)
                column.append(got)
            columns.append(jnp.concatenate(column, axis=0))
        high, low = split(jnp.concatenate(columns, axis=1))
        k_rows = slice(pair * 2 * T, (pair + 1) * 2 * T)
        term = (
            jnp.dot(high, sy[0, k_rows], preferred_element_type=f32)
            + jnp.dot(low, sy[0, k_rows], preferred_element_type=f32)
            + jnp.dot(high, sy[1, k_rows], preferred_element_type=f32)
        )
        along_y = term if along_y is None else along_y + term
    out_ref[...] = along_y * wgt[...]

    for copy in halo:
        copy.wait_send()
    pltpu.make_async_copy(rmsg.at[pl.ds(0, NG - 1)], rmsg.at[pl.ds(0, NG - 1)], msend).wait()
    for k in range(len(PIECES)):
        for kind in range(4):
            for way in range(2):
                send(k, way, kind).wait_send()
    pltpu.make_async_copy(rv.at[others], rv.at[others], asend).wait()


def per_device(orbitals, potentials, local_potential, shifts):
    lz, sx, sy = tables()
    anywhere = pl.BlockSpec(memory_space=pl.ANY)
    field = pltpu.VMEM((NF, SLAB, T), f32)
    dma = pltpu.SemaphoreType.DMA
    out = pl.pallas_call(
        kernel,
        out_shape=jax.ShapeDtypeStruct((PK * KX, NY), f32),
        in_specs=[anywhere, anywhere, anywhere, pl.BlockSpec(memory_space=pltpu.SMEM)] + [anywhere] * 3,
        out_specs=pl.BlockSpec(memory_space=pltpu.VMEM),
        scratch_shapes=[
            pltpu.VMEM((ROWS, NL * NZ, NX), f32),
            pltpu.VMEM((ROWS, NPOT * NZ, NX), f32),
            pltpu.VMEM((ROWS, NZ, NX), f32),
            pltpu.VMEM((NB * PK, NPOT * 3 * NZ), bf16),
            pltpu.VMEM((2, NX, NX), bf16),
            pltpu.VMEM((2, NY, NY), bf16),
            field,
            field,
            field,
            pltpu.VMEM((NF, 8, T), f32),
            pltpu.VMEM((NL, 4, 8, T), f32),
            pltpu.VMEM((1, T), f32),
            pltpu.VMEM((NG, 1, T), f32),
            pltpu.VMEM((NL, SLAB, T), f32),
            pltpu.VMEM((NL, SLAB, T), f32),
            pltpu.VMEM((NB, NR, PK, NX), f32),
            pltpu.VMEM((2, 4, NR, PK, NX), f32),
            pltpu.VMEM((NR * PK, NX), f32),
            pltpu.VMEM((NG, KX, NR * PK), f32),
            pltpu.VMEM((NG, KX, NR * PK), f32),
            pltpu.VMEM((PK * KX, NY), f32),
            dma((3, NR // GROUP)),
            dma((3,)),
            dma((2, 3)),
            dma((2, 3)),
            dma,
            dma,
            dma((2, 4, len(PIECES))),
            dma((2, 4, len(PIECES))),
            dma,
            dma,
        ],
        compiler_params=pltpu.CompilerParams(
            collective_id=0, has_side_effects=True, vmem_limit_bytes=56 * 1024 * 1024
        ),
    )(
        orbitals.reshape(NL * NZ, NR, NX),
        potentials.reshape(NPOT * NZ, NR, NX),
        local_potential,
        shifts,
        jnp.asarray(lz),
        jnp.asarray(sx),
        jnp.asarray(sy),
    )
    return out.reshape(NPOT, KZ, KX, NY)


def solution(mesh):
    placed = (
        P("band", None, "gy", None),
        P(None, None, "gy", None),
        P(None, "gy", None),
        P("band"),
    )
    return jax.shard_map(
        per_device,
        mesh=mesh,
        in_specs=placed,
        out_specs=P(None, "band", "gy", None),
        check_vma=False,
    )
```

```python
import jax
import jax.numpy as jnp
import numpy as np
from jax import lax
from jax.experimental import pallas as pl
from jax.experimental.pallas import tpu as pltpu
from jax.sharding import PartitionSpec as P

NX, NY, NZ, NPOT, SWEEPS, NORB = 256, 512, 32, 2, 3, 32
NB, NG = 8, 32
NL = NORB // NB
NR = NY // NG
NF = NL * NPOT
H = 3
KZ, KX = NZ // NB, NX // NG
PK = NPOT * KZ
T = 128
ZO = 8
ROWS = NR + 2 * H
ZB = ZO + NZ
SLAB = ROWS * 2 * ZB + ZO
PIECES = ((3, 3), (6, 3), (9, 4), (13, 3), (0, 3))
GROUP = 4
SPREAD, SCREEN = 3.5, 0.25
MESH = pl.DeviceIdType.MESH
f32, bf16 = jnp.float32, jnp.bfloat16


def sine(length):
    k = np.arange(1, length + 1, dtype=np.float64)
    return np.sqrt(2.0 / (length + 1)) * np.sin(np.pi * np.outer(k, k) / (length + 1))


def halves(table):
    high = table.astype(np.float32).astype(bf16)
    low = (table - high.astype(np.float64)).astype(np.float32).astype(bf16)
    return high, low


def tables():
    zh, zl = halves(sine(NZ))
    lz = np.zeros((NB, NPOT, KZ, NPOT, 3, NZ), bf16)
    for p in range(NPOT):
        for i, part in enumerate((zh, zh, zl)):
            lz[:, p, :, p, i, :] = part.reshape(NB, KZ, NZ)
    lz = lz.reshape(NB * PK, NPOT * 3 * NZ)
    sx = np.stack(halves(sine(NX)))
    sy = np.stack(halves(sine(NY)))
    st, y, j = np.meshgrid(np.arange(NG // 8), np.arange(NR), np.arange(8), indexing="ij")
    sy = sy[:, (NR * (8 * st + j) + y).reshape(-1), :]
    return lz, sx, sy


def split(value):
    high = value.astype(bf16)
    return high, (value - high.astype(f32)).astype(bf16)


def polynomial(shift):
    c = shift + SPREAD
    ratio = c / SPREAD
    now = 1.0 / ratio
    d, r, x = [1.0 / c], [jnp.ones_like(c)], []

    def add(a, b):
        out = []
        for i in range(max(len(a), len(b))):
            if i < len(a) and i < len(b):
                out.append(a[i] + b[i])
            else:
                out.append(a[i] if i < len(a) else b[i])
        return out

    for _ in range(SWEEPS):
        x = add(x, d)
        ad = [c * d[0]]
        for i in range(1, len(d)):
            ad.append(c * d[i] - 0.5 * d[i - 1])
        ad.append(-0.5 * d[-1])
        r = add(r, [-v for v in ad])
        after = 1.0 / (2.0 * ratio - now)
        d = add([after * now * v for v in d], [(2.0 * after / SPREAD) * v for v in r])
        now = after
    return add(x, d)


def kernel(
    orb_hbm, pot_hbm, loc_hbm, shift_ref, lz_hbm, sx_hbm, sy_hbm, out_ref,
    orbv, potv, locv, lz, sx, sy, f0, f1, f2, cf, pc, msg, rmsg,
    e0, e1, part, inbox, dv, ov, rv, wgt,
    load_sem, table_sem, hsend, hrecv, msend, mrecv, rsend, rrecv, asend, arecv,
):
    band, gy = lax.axis_index("band"), lax.axis_index("gy")

    barrier = pltpu.get_barrier_semaphore()
    for d in range(1, NG):
        pl.semaphore_signal(barrier, 1, device_id=(band, lax.rem(gy + d, NG)), device_id_type=MESH)
    for d in range(1, NB):
        pl.semaphore_signal(barrier, 1, device_id=(lax.rem(band + d, NB), gy), device_id_type=MESH)

    arrays = ((orb_hbm, orbv), (pot_hbm, potv), (loc_hbm, locv))
    for y in range(NR):
        for i, (src, dst) in enumerate(arrays):
            pltpu.make_async_copy(src.at[:, y], dst.at[H + y], load_sem.at[i, y // GROUP]).start()
    tables_in = []
    for i, (src, dst) in enumerate(((lz_hbm, lz), (sx_hbm, sx), (sy_hbm, sy))):
        tables_in.append(pltpu.make_async_copy(src, dst, table_sem.at[i]))
        tables_in[-1].start()

    zero = jnp.zeros((8, T), f32)

    def sums(r, acc):
        acc = list(acc)
        for z in range(NZ // 8):
            for x in range(2):
                cols = slice(T * x, T * (x + 1))
                pots = [potv[r, p * NZ + z * 8 : p * NZ + z * 8 + 8, cols] for p in range(NPOT)]
                for n in range(NL):
                    o = orbv[r, n * NZ + z * 8 : n * NZ + z * 8 + 8, cols]
                    q = o * o
                    for p in range(NPOT):
                        acc[p * NL + n] = acc[p * NL + n] + pots[p] * q
                    acc[NF + n] = acc[NF + n] + q
        return tuple(acc)

    acc = tuple(zero for _ in range(NF + NL))
    for g in range(NR // GROUP):
        rows = pl.ds(H + g * GROUP, GROUP)
        for i, (_, dst) in enumerate(arrays):
            pltpu.make_async_copy(dst.at[rows], dst.at[rows], load_sem.at[i, g]).wait()
        acc = lax.fori_loop(H + g * GROUP, H + (g + 1) * GROUP, sums, acc)
    lane1 = lax.broadcasted_iota(jnp.int32, (1, T), 1)
    row = jnp.zeros((1, T), f32)
    for i, a in enumerate(acc):
        total = jnp.sum(jnp.sum(a, axis=0, keepdims=True), axis=1, keepdims=True)
        row = jnp.where(lane1 == i, total, row)
    msg[...] = row

    pl.semaphore_wait(barrier, NG - 1 + NB - 1)

    for d in range(1, NG):
        pltpu.make_async_remote_copy(
            msg, rmsg.at[d], msend, mrecv,
            device_id=(band, lax.rem(gy + d, NG)), device_id_type=MESH,
        ).start()

    halo = []
    for side in range(2):
        target = lax.rem(gy + (NG - 1 if side == 0 else 1), NG)
        for i, (_, dst) in enumerate(arrays):
            width = H if i < 2 else H - 1
            if side == 0:
                src, to = pl.ds(H, width), pl.ds(H + NR, width)
            else:
                src, to = pl.ds(H + NR - width, width), pl.ds(H - width, width)
            copy = pltpu.make_async_remote_copy(
                dst.at[src], dst.at[to], hsend.at[side, i], hrecv.at[side, i],
                device_id=(band, target), device_id_type=MESH,
            )
            copy.start()
            halo.append(copy)

    def clear(i, carry):
        for f in range(NF):
            for field in (f0, f1, f2):
                field[f, pl.ds(pl.multiple_of(i * ZB, 8), ZO), :] = zero
        for n in range(NL):
            e0[n, pl.ds(pl.multiple_of(i * ZB, 8), ZO), :] = zero
        return carry

    lax.fori_loop(0, 2 * ROWS + 1, clear, 0)

    for n in range(NL):
        a = polynomial(jnp.full((8, T), shift_ref[n], f32))
        inverse = 1.0 / a[3]
        pc[n, 0] = a[2] * inverse
        pc[n, 1] = a[1] * inverse
        pc[n, 2] = a[0] * inverse
        pc[n, 3] = -4.0 * a[3]

    def index_of(shape, axis):
        return lax.broadcasted_iota(jnp.int32, shape, axis)

    shape = (PK * KX, NY)
    r_index = index_of(shape, 0)
    kz = band * KZ + lax.rem(lax.div(r_index, KX), KZ)
    kx = gy * KX + lax.rem(r_index, KX)
    qz = jnp.pi * (kz.astype(f32) + 1.0) / (NZ + 1)
    qx = jnp.pi * (kx.astype(f32) + 1.0) / (NX + 1)
    qy = jnp.pi * (index_of(shape, 1).astype(f32) + 1.0) / (NY + 1)
    wgt[...] = jnp.sqrt(4.0 * jnp.pi / (qz * qz + qx * qx + qy * qy + SCREEN))

    def whole(tile):
        return jnp.concatenate([tile] * (NZ // 8), axis=0)

    def at(r, x, shift=0):
        return pl.ds(pl.multiple_of((r * 2 + x) * ZB + ZO, 8) + shift, NZ)

    def half(ref, r, i, x):
        return ref[r, i * NZ : (i + 1) * NZ, x * T : (x + 1) * T]

    def w_of(r, x):
        return 1.0 - 2.0 * half(locv, r, 0, x)

    def source(r, mask=None):
        for x in range(2):
            pots = [half(potv, r, p, x) for p in range(NPOT)]
            for n in range(NL):
                o = half(orbv, r, n, x)
                if mask is not None:
                    o = o * mask
                for p in range(NPOT):
                    f = n * NPOT + p
                    f0[f, at(r, x), :] = (pots[p] - whole(cf[f])) * o

    lane = lax.broadcasted_iota(jnp.int32, (NZ, T), 1)
    first, last = lane == 0, lane == T - 1
    nought = jnp.zeros((NZ, T), f32)

    def near(field, f, r):
        c = [field[f, at(r, x), :] for x in range(2)]
        up = [pltpu.roll(v, 1, 1) for v in c]
        down = [pltpu.roll(v, T - 1, 1) for v in c]
        beside = [
            jnp.where(first, nought, up[0]) + jnp.where(last, down[1], down[0]),
            jnp.where(first, up[0], up[1]) + jnp.where(last, nought, down[1]),
        ]
        found = []
        for x in range(2):
            z = field[f, at(r, x, -1), :] + field[f, at(r, x, 1), :]
            y = field[f, at(r - 1, x), :] + field[f, at(r + 1, x), :]
            found.append(beside[x] + (z + y))
        return c, found

    def sweep_one(r, mask=None):
        w = [w_of(r, x) for x in range(2)]
        for n in range(NL):
            ws = [w[x] + whole(pc[n, 0]) for x in range(2)]
            for p in range(NPOT):
                f = n * NPOT + p
                c, s = near(f0, f, r)
                for x in range(2):
                    value = s[x] + ws[x] * c[x]
                    f1[f, at(r, x), :] = value if mask is None else value * mask

    def products(r):
        for x in range(2):
            pots = [half(potv, r, p, x) for p in range(NPOT)]
            for n in range(NL):
                o = half(orbv, r, n, x)
                e0[n, at(r, x), :] = o
                for p in range(NPOT):
                    f0[n * NPOT + p, at(r, x), :] = pots[p] * o

    def sweep_products(r):
        w = [w_of(r, x) for x in range(2)]
        for n in range(NL):
            ws = [w[x] + whole(pc[n, 0]) for x in range(2)]
            for src, dst, f in ((f0, f1, n * NPOT), (f0, f1, n * NPOT + 1), (e0, e1, n)):
                c, s = near(src, f, r)
                for x in range(2):
                    dst[f, at(r, x), :] = s[x] + ws[x] * c[x]

    def settle_source(r):
        for x in range(2):
            for n in range(NL):
                o = e0[n, at(r, x), :]
                for p in range(NPOT):
                    f = n * NPOT + p
                    f0[f, at(r, x), :] = f0[f, at(r, x), :] - whole(cf[f]) * o

    def settle_first(r):
        for x in range(2):
            for n in range(NL):
                o = e1[n, at(r, x), :]
                for p in range(NPOT):
                    f = n * NPOT + p
                    f1[f, at(r, x), :] = f1[f, at(r, x), :] - whole(cf[f]) * o

    def sweep_two(r, mask=None):
        w = [w_of(r, x) for x in range(2)]
        for n in range(NL):
            beta = whole(pc[n, 1])
            for p in range(NPOT):
                f = n * NPOT + p
                c, s = near(f1, f, r)
                for x in range(2):
                    value = s[x] + w[x] * c[x] + beta * f0[f, at(r, x), :]
                    f2[f, at(r, x), :] = value if mask is None else value * mask

    def last_sweep(r):
        w = [w_of(r, x) for x in range(2)]
        density = [[None, None] for _ in range(NPOT)]
        for n in range(NL):
            beta, gamma = whole(pc[n, 2]), whole(pc[n, 3])
            orbs = [half(orbv, r, n, x) * gamma for x in range(2)]
            for p in range(NPOT):
                f = n * NPOT + p
                c, s = near(f2, f, r)
                for x in range(2):
                    value = s[x] + w[x] * c[x] + beta * f0[f, at(r, x), :]
                    term = orbs[x] * value
                    old = density[p][x]
                    density[p][x] = term if old is None else old + term
        for x in range(2):
            stack = []
            for p in range(NPOT):
                high, low = split(density[p][x])
                stack += [high, low, high]
            along_z = jnp.dot(lz[...], jnp.concatenate(stack, axis=0), preferred_element_type=f32)
            for b in range(NB):
                part[b, r - H, :, T * x : T * (x + 1)] = along_z[b * PK : (b + 1) * PK, :]

    def send(k, way, kind):
        low, count = PIECES[k]
        far, reach = ((4, 2), (3, 1), (1, 1), (2, 2))[kind]
        rows = part_rows(k, way) if kind == 0 else pl.ds(low, count)
        chunk = lax.rem(band + (far if way == 0 else NB - far), NB)
        to = lax.rem(band + (reach if way == 0 else NB - reach), NB)
        return pltpu.make_async_remote_copy(
            part.at[chunk, rows], inbox.at[way, kind, rows], rsend.at[way, kind, k], rrecv.at[way, kind, k],
            device_id=(to, gy), device_id_type=MESH,
        )

    def part_rows(k, way):
        low, count = PIECES[k]
        cut = (count + (k % 2)) // 2
        return pl.ds(low, cut) if way == 0 else pl.ds(low + cut, count - cut)

    def begin(k):
        for kind in (0, 1, 2):
            for way in range(2):
                send(k, way, kind).start()

    def middle(k):
        low, count = PIECES[k]
        rows = pl.ds(low, count)
        for way in range(2):
            send(k, way, 0).wait_recv()
            send(k, way, 1).wait_recv()
            chunk = lax.rem(band + (2 if way == 0 else NB - 2), NB)
            part[chunk, rows] = part[chunk, rows] + inbox[way, 1, rows]
            some = part_rows(k, way)
            part[chunk, some] = part[chunk, some] + inbox[way, 0, some]
            send(k, way, 3).start()

    def finish(k):
        low, count = PIECES[k]
        rows = pl.ds(low, count)
        for kind in (2, 3):
            for way in range(2):
                send(k, way, kind).wait_recv()
        value = part[band, rows] + ((inbox[0, 2, rows] + inbox[1, 2, rows]) + (inbox[0, 3, rows] + inbox[1, 3, rows]))
        dv[low * PK : (low + count) * PK, :] = value.reshape(count * PK, NX)

    def loop(low, high, body):
        def step(r, carry):
            body(r)
            return carry

        if high == low + 1:
            body(low)
        else:
            lax.fori_loop(low, high, step, 0)

    loop(H, H + NR, products)
    loop(H + 1, H + NR - 1, sweep_products)

    pltpu.make_async_copy(rmsg.at[pl.ds(0, NG - 1)], rmsg.at[pl.ds(0, NG - 1)], mrecv).wait()
    total = msg[...]
    for d in range(1, NG):
        total = total + rmsg[d]
    for n in range(NL):
        norm = total[:, NF + n : NF + n + 1]
        for p in range(NPOT):
            value = total[:, p * NL + n : p * NL + n + 1] / norm
            cf[n * NPOT + p] = jnp.broadcast_to(value, (8, T))

    done = [H, H + 1, H + 2, H + 3]
    for k in range(3):
        end = H + PIECES[k][0] + PIECES[k][1]
        for i, body in enumerate((settle_source, settle_first, sweep_two, last_sweep)):
            stop = min(end + 3 - i, H + NR - i)
            loop(done[i], stop, body)
            done[i] = stop
            if k == 0 and i == 2:
                tables_in[0].wait()
            if k == 2 and i == 2:
                middle(0)
        begin(k)

    low_mask = jnp.where(gy == 0, 0.0, 1.0).astype(f32)
    high_mask = jnp.where(gy == NG - 1, 0.0, 1.0).astype(f32)
    for copy in halo:
        copy.wait_recv()
    top = H + NR
    loop(top, top + 3, lambda r: source(r, high_mask))
    loop(top - 1, top, sweep_one)
    loop(top, top + 2, lambda r: sweep_one(r, high_mask))
    loop(top - 2, top, sweep_two)
    loop(top, top + 1, lambda r: sweep_two(r, high_mask))
    loop(top - 3, top, last_sweep)
    begin(3)
    middle(1)
    loop(0, H, lambda r: source(r, low_mask))
    loop(1, H, lambda r: sweep_one(r, low_mask))
    loop(H, H + 1, sweep_one)
    loop(H - 1, H, lambda r: sweep_two(r, low_mask))
    loop(H, H + 2, sweep_two)
    middle(2)
    loop(H, H + 3, last_sweep)
    begin(4)
    middle(3)
    finish(0)
    finish(1)
    finish(2)
    middle(4)
    finish(3)
    finish(4)

    tables_in[1].wait()
    high, low = split(dv[...])

    def by_rows(a, b):
        return lax.dot_general(a, b, (((1,), (1,)), ((), ())), preferred_element_type=f32)

    along_x = by_rows(sx[0], high) + by_rows(sx[0], low) + by_rows(sx[1], high)
    ov[...] = along_x.reshape(NG, KX, NR * PK)

    for d in range(1, NG):
        target = lax.rem(gy + d, NG)
        pltpu.make_async_remote_copy(
            ov.at[target], rv.at[gy], asend, arecv, device_id=(band, target), device_id_type=MESH
        ).start()
    rv[gy] = ov[gy]
    tables_in[2].wait()

    others = pl.ds(0, NG - 1)
    pltpu.make_async_copy(rv.at[others], rv.at[others], arecv).wait()

    lane8 = lax.rem(lax.broadcasted_iota(jnp.int32, (KX, T), 1), 8)
    along_y = None
    for pair in range(NG // 16):
        columns = []
        for st in (2 * pair, 2 * pair + 1):
            tiles = [rv[st * 8 + j] for j in range(8)]
            column = []
            for pk in range(PK):
                got = None
                for j in range(8):
                    shift = (j - pk) % T
                    moved = tiles[j] if shift == 0 else pltpu.roll(tiles[j], shift, 1)
                    got = moved if got is None else jnp.where(lane8 == j, moved, got)
                column.append(got)
            columns.append(jnp.concatenate(column, axis=0))
        high, low = split(jnp.concatenate(columns, axis=1))
        k_rows = slice(pair * 2 * T, (pair + 1) * 2 * T)
        term = (
            jnp.dot(high, sy[0, k_rows], preferred_element_type=f32)
            + jnp.dot(low, sy[0, k_rows], preferred_element_type=f32)
            + jnp.dot(high, sy[1, k_rows], preferred_element_type=f32)
        )
        along_y = term if along_y is None else along_y + term
    out_ref[...] = along_y * wgt[...]

    for copy in halo:
        copy.wait_send()
    pltpu.make_async_copy(rmsg.at[pl.ds(0, NG - 1)], rmsg.at[pl.ds(0, NG - 1)], msend).wait()
    for k in range(len(PIECES)):
        for kind in range(4):
            for way in range(2):
                send(k, way, kind).wait_send()
    pltpu.make_async_copy(rv.at[others], rv.at[others], asend).wait()


def per_device(orbitals, potentials, local_potential, shifts):
    lz, sx, sy = tables()
    anywhere = pl.BlockSpec(memory_space=pl.ANY)
    field = pltpu.VMEM((NF, SLAB, T), f32)
    dma = pltpu.SemaphoreType.DMA
    out = pl.pallas_call(
        kernel,
        out_shape=jax.ShapeDtypeStruct((PK * KX, NY), f32),
        in_specs=[anywhere, anywhere, anywhere, pl.BlockSpec(memory_space=pltpu.SMEM)] + [anywhere] * 3,
        out_specs=pl.BlockSpec(memory_space=pltpu.VMEM),
        scratch_shapes=[
            pltpu.VMEM((ROWS, NL * NZ, NX), f32),
            pltpu.VMEM((ROWS, NPOT * NZ, NX), f32),
            pltpu.VMEM((ROWS, NZ, NX), f32),
            pltpu.VMEM((NB * PK, NPOT * 3 * NZ), bf16),
            pltpu.VMEM((2, NX, NX), bf16),
            pltpu.VMEM((2, NY, NY), bf16),
            field,
            field,
            field,
            pltpu.VMEM((NF, 8, T), f32),
            pltpu.VMEM((NL, 4, 8, T), f32),
            pltpu.VMEM((1, T), f32),
            pltpu.VMEM((NG, 1, T), f32),
            pltpu.VMEM((NL, SLAB, T), f32),
            pltpu.VMEM((NL, SLAB, T), f32),
            pltpu.VMEM((NB, NR, PK, NX), f32),
            pltpu.VMEM((2, 4, NR, PK, NX), f32),
            pltpu.VMEM((NR * PK, NX), f32),
            pltpu.VMEM((NG, KX, NR * PK), f32),
            pltpu.VMEM((NG, KX, NR * PK), f32),
            pltpu.VMEM((PK * KX, NY), f32),
            dma((3, NR // GROUP)),
            dma((3,)),
            dma((2, 3)),
            dma((2, 3)),
            dma,
            dma,
            dma((2, 4, len(PIECES))),
            dma((2, 4, len(PIECES))),
            dma,
            dma,
        ],
        compiler_params=pltpu.CompilerParams(
            collective_id=0, has_side_effects=True, vmem_limit_bytes=56 * 1024 * 1024
        ),
    )(
        orbitals.reshape(NL * NZ, NR, NX),
        potentials.reshape(NPOT * NZ, NR, NX),
        local_potential,
        shifts,
        jnp.asarray(lz),
        jnp.asarray(sx),
        jnp.asarray(sy),
    )
    return out.reshape(NPOT, KZ, KX, NY)


def solution(mesh):
    placed = (
        P("band", None, "gy", None),
        P(None, None, "gy", None),
        P(None, "gy", None),
        P("band"),
    )
    return jax.shard_map(
        per_device,
        mesh=mesh,
        in_specs=placed,
        out_specs=P(None, "band", "gy", None),
        check_vma=False,
    )
```

```python
import jax
import jax.numpy as jnp
import numpy as np
from jax import lax
from jax.experimental import pallas as pl
from jax.experimental.pallas import tpu as pltpu
from jax.sharding import PartitionSpec as P

NX, NY, NZ, NPOT, SWEEPS, NORB = 256, 512, 32, 2, 3, 32
NB, NG = 8, 32
NL = NORB // NB
NR = NY // NG
NF = NL * NPOT
H = 3
KZ, KX = NZ // NB, NX // NG
PK = NPOT * KZ
T = 128
ZO = 8
ROWS = NR + 2 * H
ZB = ZO + NZ
SLAB = ROWS * 2 * ZB + ZO
PIECES = ((3, 3), (6, 3), (9, 4), (13, 3), (0, 3))
FAR_FIRST = sorted(range(1, NG), key=lambda d: -(min(d // 8, 4 - d // 8) + min(d % 8 // 2, 4 - d % 8 // 2)))
GROUP = 4
SPREAD, SCREEN = 3.5, 0.25
MESH = pl.DeviceIdType.MESH
f32, bf16 = jnp.float32, jnp.bfloat16


def sine(length):
    k = np.arange(1, length + 1, dtype=np.float64)
    return np.sqrt(2.0 / (length + 1)) * np.sin(np.pi * np.outer(k, k) / (length + 1))


def halves(table):
    high = table.astype(np.float32).astype(bf16)
    low = (table - high.astype(np.float64)).astype(np.float32).astype(bf16)
    return high, low


def tables():
    zh, zl = halves(sine(NZ))
    lz = np.zeros((NB, NPOT, KZ, NPOT, 3, NZ), bf16)
    for p in range(NPOT):
        for i, part in enumerate((zh, zh, zl)):
            lz[:, p, :, p, i, :] = part.reshape(NB, KZ, NZ)
    lz = lz.reshape(NB * PK, NPOT * 3 * NZ)
    sx = np.stack(halves(sine(NX)))
    sy = np.stack(halves(sine(NY)))
    st, y, j = np.meshgrid(np.arange(NG // 8), np.arange(NR), np.arange(8), indexing="ij")
    sy = sy[:, (NR * (8 * st + j) + y).reshape(-1), :]
    return lz, sx, sy


def split(value):
    high = value.astype(bf16)
    return high, (value - high.astype(f32)).astype(bf16)


def polynomial(shift):
    c = shift + SPREAD
    ratio = c / SPREAD
    now = 1.0 / ratio
    d, r, x = [1.0 / c], [jnp.ones_like(c)], []

    def add(a, b):
        out = []
        for i in range(max(len(a), len(b))):
            if i < len(a) and i < len(b):
                out.append(a[i] + b[i])
            else:
                out.append(a[i] if i < len(a) else b[i])
        return out

    for _ in range(SWEEPS):
        x = add(x, d)
        ad = [c * d[0]]
        for i in range(1, len(d)):
            ad.append(c * d[i] - 0.5 * d[i - 1])
        ad.append(-0.5 * d[-1])
        r = add(r, [-v for v in ad])
        after = 1.0 / (2.0 * ratio - now)
        d = add([after * now * v for v in d], [(2.0 * after / SPREAD) * v for v in r])
        now = after
    return add(x, d)


def kernel(
    orb_hbm, pot_hbm, loc_hbm, shift_ref, lz_hbm, sx_hbm, sy_hbm, out_ref,
    orbv, potv, locv, lz, sx, sy, f0, f1, f2, cf, pc, msg, rmsg,
    e0, e1, part, inbox, dv, ov, rv, wgt,
    load_sem, table_sem, hsend, hrecv, msend, mrecv, rsend, rrecv, asend, arecv,
):
    band, gy = lax.axis_index("band"), lax.axis_index("gy")

    arrays = ((orb_hbm, orbv), (pot_hbm, potv), (loc_hbm, locv))

    def load(low, high):
        for y in range(low, high):
            for i, (src, dst) in enumerate(arrays):
                pltpu.make_async_copy(src.at[:, y], dst.at[H + y], load_sem.at[i, y // GROUP]).start()

    load(0, GROUP)
    barrier = pltpu.get_barrier_semaphore()
    for d in FAR_FIRST:
        pl.semaphore_signal(barrier, 1, device_id=(band, lax.rem(gy + d, NG)), device_id_type=MESH)
    for d in range(1, NB):
        pl.semaphore_signal(barrier, 1, device_id=(lax.rem(band + d, NB), gy), device_id_type=MESH)

    load(GROUP, NR)
    tables_in = []
    for i, (src, dst) in enumerate(((lz_hbm, lz), (sx_hbm, sx), (sy_hbm, sy))):
        tables_in.append(pltpu.make_async_copy(src, dst, table_sem.at[i]))
        tables_in[-1].start()

    zero = jnp.zeros((8, T), f32)

    def sums(r, acc):
        acc = list(acc)
        for z in range(NZ // 8):
            for x in range(2):
                cols = slice(T * x, T * (x + 1))
                pots = [potv[r, p * NZ + z * 8 : p * NZ + z * 8 + 8, cols] for p in range(NPOT)]
                for n in range(NL):
                    o = orbv[r, n * NZ + z * 8 : n * NZ + z * 8 + 8, cols]
                    q = o * o
                    for p in range(NPOT):
                        acc[p * NL + n] = acc[p * NL + n] + pots[p] * q
                    acc[NF + n] = acc[NF + n] + q
        return tuple(acc)

    acc = tuple(zero for _ in range(NF + NL))
    for g in range(NR // GROUP):
        rows = pl.ds(H + g * GROUP, GROUP)
        for i, (_, dst) in enumerate(arrays):
            pltpu.make_async_copy(dst.at[rows], dst.at[rows], load_sem.at[i, g]).wait()
        acc = lax.fori_loop(H + g * GROUP, H + (g + 1) * GROUP, sums, acc)
    lane1 = lax.broadcasted_iota(jnp.int32, (1, T), 1)
    row = jnp.zeros((1, T), f32)
    for i, a in enumerate(acc):
        total = jnp.sum(jnp.sum(a, axis=0, keepdims=True), axis=1, keepdims=True)
        row = jnp.where(lane1 == i, total, row)
    msg[...] = row

    pl.semaphore_wait(barrier, NG - 1 + NB - 1)

    for d in FAR_FIRST:
        pltpu.make_async_remote_copy(
            msg, rmsg.at[d], msend, mrecv,
            device_id=(band, lax.rem(gy + d, NG)), device_id_type=MESH,
        ).start()

    halo = []
    for side in range(2):
        target = lax.rem(gy + (NG - 1 if side == 0 else 1), NG)
        for i, (_, dst) in enumerate(arrays):
            width = H if i < 2 else H - 1
            if side == 0:
                src, to = pl.ds(H, width), pl.ds(H + NR, width)
            else:
                src, to = pl.ds(H + NR - width, width), pl.ds(H - width, width)
            copy = pltpu.make_async_remote_copy(
                dst.at[src], dst.at[to], hsend.at[side, i], hrecv.at[side, i],
                device_id=(band, target), device_id_type=MESH,
            )
            copy.start()
            halo.append(copy)

    def clear(i, carry):
        for f in range(NF):
            for field in (f0, f1, f2):
                field[f, pl.ds(pl.multiple_of(i * ZB, 8), ZO), :] = zero
        for n in range(NL):
            e0[n, pl.ds(pl.multiple_of(i * ZB, 8), ZO), :] = zero
        return carry

    lax.fori_loop(0, 2 * ROWS + 1, clear, 0)

    for n in range(NL):
        a = polynomial(jnp.full((8, T), shift_ref[n], f32))
        inverse = 1.0 / a[3]
        pc[n, 0] = a[2] * inverse
        pc[n, 1] = a[1] * inverse
        pc[n, 2] = a[0] * inverse
        pc[n, 3] = -4.0 * a[3]

    def index_of(shape, axis):
        return lax.broadcasted_iota(jnp.int32, shape, axis)

    shape = (PK * KX, NY)
    r_index = index_of(shape, 0)
    kz = band * KZ + lax.rem(lax.div(r_index, KX), KZ)
    kx = gy * KX + lax.rem(r_index, KX)
    qz = jnp.pi * (kz.astype(f32) + 1.0) / (NZ + 1)
    qx = jnp.pi * (kx.astype(f32) + 1.0) / (NX + 1)
    qy = jnp.pi * (index_of(shape, 1).astype(f32) + 1.0) / (NY + 1)
    wgt[...] = jnp.sqrt(4.0 * jnp.pi / (qz * qz + qx * qx + qy * qy + SCREEN))

    def whole(tile):
        return jnp.concatenate([tile] * (NZ // 8), axis=0)

    def at(r, x, shift=0):
        return pl.ds(pl.multiple_of((r * 2 + x) * ZB + ZO, 8) + shift, NZ)

    def half(ref, r, i, x):
        return ref[r, i * NZ : (i + 1) * NZ, x * T : (x + 1) * T]

    def w_of(r, x):
        return 1.0 - 2.0 * half(locv, r, 0, x)

    def source(r, mask=None):
        for x in range(2):
            pots = [half(potv, r, p, x) for p in range(NPOT)]
            for n in range(NL):
                o = half(orbv, r, n, x)
                if mask is not None:
                    o = o * mask
                for p in range(NPOT):
                    f = n * NPOT + p
                    f0[f, at(r, x), :] = (pots[p] - whole(cf[f])) * o

    lane = lax.broadcasted_iota(jnp.int32, (NZ, T), 1)
    first, last = lane == 0, lane == T - 1
    nought = jnp.zeros((NZ, T), f32)

    def near(field, f, r):
        c = [field[f, at(r, x), :] for x in range(2)]
        up = [pltpu.roll(v, 1, 1) for v in c]
        down = [pltpu.roll(v, T - 1, 1) for v in c]
        beside = [
            jnp.where(first, nought, up[0]) + jnp.where(last, down[1], down[0]),
            jnp.where(first, up[0], up[1]) + jnp.where(last, nought, down[1]),
        ]
        found = []
        for x in range(2):
            z = field[f, at(r, x, -1), :] + field[f, at(r, x, 1), :]
            y = field[f, at(r - 1, x), :] + field[f, at(r + 1, x), :]
            found.append(beside[x] + (z + y))
        return c, found

    def sweep_one(r, mask=None):
        w = [w_of(r, x) for x in range(2)]
        for n in range(NL):
            ws = [w[x] + whole(pc[n, 0]) for x in range(2)]
            for p in range(NPOT):
                f = n * NPOT + p
                c, s = near(f0, f, r)
                for x in range(2):
                    value = s[x] + ws[x] * c[x]
                    f1[f, at(r, x), :] = value if mask is None else value * mask

    def products(r):
        for x in range(2):
            pots = [half(potv, r, p, x) for p in range(NPOT)]
            for n in range(NL):
                o = half(orbv, r, n, x)
                e0[n, at(r, x), :] = o
                for p in range(NPOT):
                    f0[n * NPOT + p, at(r, x), :] = pots[p] * o

    def sweep_products(r):
        w = [w_of(r, x) for x in range(2)]
        for n in range(NL):
            ws = [w[x] + whole(pc[n, 0]) for x in range(2)]
            for src, dst, f in ((f0, f1, n * NPOT), (f0, f1, n * NPOT + 1), (e0, e1, n)):
                c, s = near(src, f, r)
                for x in range(2):
                    dst[f, at(r, x), :] = s[x] + ws[x] * c[x]

    def settle_source(r):
        for x in range(2):
            for n in range(NL):
                o = e0[n, at(r, x), :]
                for p in range(NPOT):
                    f = n * NPOT + p
                    f0[f, at(r, x), :] = f0[f, at(r, x), :] - whole(cf[f]) * o

    def settle_first(r):
        for x in range(2):
            for n in range(NL):
                o = e1[n, at(r, x), :]
                for p in range(NPOT):
                    f = n * NPOT + p
                    f1[f, at(r, x), :] = f1[f, at(r, x), :] - whole(cf[f]) * o

    def sweep_two(r, mask=None):
        w = [w_of(r, x) for x in range(2)]
        for n in range(NL):
            beta = whole(pc[n, 1])
            for p in range(NPOT):
                f = n * NPOT + p
                c, s = near(f1, f, r)
                for x in range(2):
                    value = s[x] + w[x] * c[x] + beta * f0[f, at(r, x), :]
                    f2[f, at(r, x), :] = value if mask is None else value * mask

    def last_sweep(r):
        w = [w_of(r, x) for x in range(2)]
        density = [[None, None] for _ in range(NPOT)]
        for n in range(NL):
            beta, gamma = whole(pc[n, 2]), whole(pc[n, 3])
            orbs = [half(orbv, r, n, x) * gamma for x in range(2)]
            for p in range(NPOT):
                f = n * NPOT + p
                c, s = near(f2, f, r)
                for x in range(2):
                    value = s[x] + w[x] * c[x] + beta * f0[f, at(r, x), :]
                    term = orbs[x] * value
                    old = density[p][x]
                    density[p][x] = term if old is None else old + term
        for x in range(2):
            stack = []
            for p in range(NPOT):
                high, low = split(density[p][x])
                stack += [high, low, high]
            along_z = jnp.dot(lz[...], jnp.concatenate(stack, axis=0), preferred_element_type=f32)
            for b in range(NB):
                part[b, r - H, :, T * x : T * (x + 1)] = along_z[b * PK : (b + 1) * PK, :]

    def send(k, way, kind):
        low, count = PIECES[k]
        far, reach = ((4, 2), (3, 1), (1, 1), (2, 2))[kind]
        rows = part_rows(k, way) if kind == 0 else pl.ds(low, count)
        chunk = lax.rem(band + (far if way == 0 else NB - far), NB)
        to = lax.rem(band + (reach if way == 0 else NB - reach), NB)
        return pltpu.make_async_remote_copy(
            part.at[chunk, rows], inbox.at[way, kind, rows], rsend.at[way, kind, k], rrecv.at[way, kind, k],
            device_id=(to, gy), device_id_type=MESH,
        )

    def part_rows(k, way):
        low, count = PIECES[k]
        cut = (count + (k % 2)) // 2
        return pl.ds(low, cut) if way == 0 else pl.ds(low + cut, count - cut)

    def begin(k):
        for kind in (0, 1, 2):
            for way in range(2):
                send(k, way, kind).start()

    def middle(k):
        low, count = PIECES[k]
        rows = pl.ds(low, count)
        for way in range(2):
            send(k, way, 0).wait_recv()
            send(k, way, 1).wait_recv()
            chunk = lax.rem(band + (2 if way == 0 else NB - 2), NB)
            part[chunk, rows] = part[chunk, rows] + inbox[way, 1, rows]
            some = part_rows(k, way)
            part[chunk, some] = part[chunk, some] + inbox[way, 0, some]
            send(k, way, 3).start()

    def finish(k):
        low, count = PIECES[k]
        rows = pl.ds(low, count)
        for kind in (2, 3):
            for way in range(2):
                send(k, way, kind).wait_recv()
        value = part[band, rows] + ((inbox[0, 2, rows] + inbox[1, 2, rows]) + (inbox[0, 3, rows] + inbox[1, 3, rows]))
        dv[low * PK : (low + count) * PK, :] = value.reshape(count * PK, NX)

    def loop(low, high, body):
        def step(r, carry):
            body(r)
            return carry

        if high == low + 1:
            body(low)
        else:
            lax.fori_loop(low, high, step, 0)

    loop(H, H + NR, products)
    loop(H + 1, H + NR - 1, sweep_products)

    pltpu.make_async_copy(rmsg.at[pl.ds(0, NG - 1)], rmsg.at[pl.ds(0, NG - 1)], mrecv).wait()
    total = msg[...]
    for d in range(1, NG):
        total = total + rmsg[d]
    for n in range(NL):
        norm = total[:, NF + n : NF + n + 1]
        for p in range(NPOT):
            value = total[:, p * NL + n : p * NL + n + 1] / norm
            cf[n * NPOT + p] = jnp.broadcast_to(value, (8, T))

    done = [H, H + 1, H + 2, H + 3]
    for k in range(3):
        end = H + PIECES[k][0] + PIECES[k][1]
        for i, body in enumerate((settle_source, settle_first, sweep_two, last_sweep)):
            stop = min(end + 3 - i, H + NR - i)
            loop(done[i], stop, body)
            done[i] = stop
            if k == 0 and i == 2:
                tables_in[0].wait()
            if k == 2 and i == 2:
                middle(0)
        begin(k)

    low_mask = jnp.where(gy == 0, 0.0, 1.0).astype(f32)
    high_mask = jnp.where(gy == NG - 1, 0.0, 1.0).astype(f32)
    for copy in halo:
        copy.wait_recv()
    top = H + NR
    loop(top, top + 3, lambda r: source(r, high_mask))
    loop(top - 1, top, sweep_one)
    loop(top, top + 2, lambda r: sweep_one(r, high_mask))
    loop(top - 2, top, sweep_two)
    loop(top, top + 1, lambda r: sweep_two(r, high_mask))
    middle(1)
    loop(top - 3, top, last_sweep)
    begin(3)
    loop(0, H, lambda r: source(r, low_mask))
    loop(1, H, lambda r: sweep_one(r, low_mask))
    loop(H, H + 1, sweep_one)
    loop(H - 1, H, lambda r: sweep_two(r, low_mask))
    loop(H, H + 2, sweep_two)
    middle(2)
    loop(H, H + 3, last_sweep)
    begin(4)
    middle(3)
    finish(0)
    finish(1)
    middle(4)
    finish(2)
    finish(3)
    finish(4)

    tables_in[1].wait()
    high, low = split(dv[...])

    def by_rows(a, b):
        return lax.dot_general(a, b, (((1,), (1,)), ((), ())), preferred_element_type=f32)

    along_x = by_rows(sx[0], high) + by_rows(sx[0], low) + by_rows(sx[1], high)
    ov[...] = along_x.reshape(NG, KX, NR * PK)

    for d in FAR_FIRST:
        target = lax.rem(gy + d, NG)
        pltpu.make_async_remote_copy(
            ov.at[target], rv.at[gy], asend, arecv, device_id=(band, target), device_id_type=MESH
        ).start()
    rv[gy] = ov[gy]
    tables_in[2].wait()

    others = pl.ds(0, NG - 1)
    pltpu.make_async_copy(rv.at[others], rv.at[others], arecv).wait()

    lane8 = lax.rem(lax.broadcasted_iota(jnp.int32, (KX, T), 1), 8)
    along_y = None
    for pair in range(NG // 16):
        columns = []
        for st in (2 * pair, 2 * pair + 1):
            tiles = [rv[st * 8 + j] for j in range(8)]
            column = []
            for pk in range(PK):
                got = None
                for j in range(8):
                    shift = (j - pk) % T
                    moved = tiles[j] if shift == 0 else pltpu.roll(tiles[j], shift, 1)
                    got = moved if got is None else jnp.where(lane8 == j, moved, got)
                column.append(got)
            columns.append(jnp.concatenate(column, axis=0))
        high, low = split(jnp.concatenate(columns, axis=1))
        k_rows = slice(pair * 2 * T, (pair + 1) * 2 * T)
        term = (
            jnp.dot(high, sy[0, k_rows], preferred_element_type=f32)
            + jnp.dot(low, sy[0, k_rows], preferred_element_type=f32)
            + jnp.dot(high, sy[1, k_rows], preferred_element_type=f32)
        )
        along_y = term if along_y is None else along_y + term
    out_ref[...] = along_y * wgt[...]

    for copy in halo:
        copy.wait_send()
    pltpu.make_async_copy(rmsg.at[pl.ds(0, NG - 1)], rmsg.at[pl.ds(0, NG - 1)], msend).wait()
    for k in range(len(PIECES)):
        for kind in range(4):
            for way in range(2):
                send(k, way, kind).wait_send()
    pltpu.make_async_copy(rv.at[others], rv.at[others], asend).wait()


def per_device(orbitals, potentials, local_potential, shifts):
    lz, sx, sy = tables()
    anywhere = pl.BlockSpec(memory_space=pl.ANY)
    field = pltpu.VMEM((NF, SLAB, T), f32)
    dma = pltpu.SemaphoreType.DMA
    out = pl.pallas_call(
        kernel,
        out_shape=jax.ShapeDtypeStruct((PK * KX, NY), f32),
        in_specs=[anywhere, anywhere, anywhere, pl.BlockSpec(memory_space=pltpu.SMEM)] + [anywhere] * 3,
        out_specs=pl.BlockSpec(memory_space=pltpu.VMEM),
        scratch_shapes=[
            pltpu.VMEM((ROWS, NL * NZ, NX), f32),
            pltpu.VMEM((ROWS, NPOT * NZ, NX), f32),
            pltpu.VMEM((ROWS, NZ, NX), f32),
            pltpu.VMEM((NB * PK, NPOT * 3 * NZ), bf16),
            pltpu.VMEM((2, NX, NX), bf16),
            pltpu.VMEM((2, NY, NY), bf16),
            field,
            field,
            field,
            pltpu.VMEM((NF, 8, T), f32),
            pltpu.VMEM((NL, 4, 8, T), f32),
            pltpu.VMEM((1, T), f32),
            pltpu.VMEM((NG, 1, T), f32),
            pltpu.VMEM((NL, SLAB, T), f32),
            pltpu.VMEM((NL, SLAB, T), f32),
            pltpu.VMEM((NB, NR, PK, NX), f32),
            pltpu.VMEM((2, 4, NR, PK, NX), f32),
            pltpu.VMEM((NR * PK, NX), f32),
            pltpu.VMEM((NG, KX, NR * PK), f32),
            pltpu.VMEM((NG, KX, NR * PK), f32),
            pltpu.VMEM((PK * KX, NY), f32),
            dma((3, NR // GROUP)),
            dma((3,)),
            dma((2, 3)),
            dma((2, 3)),
            dma,
            dma,
            dma((2, 4, len(PIECES))),
            dma((2, 4, len(PIECES))),
            dma,
            dma,
        ],
        compiler_params=pltpu.CompilerParams(
            collective_id=0, has_side_effects=True, vmem_limit_bytes=56 * 1024 * 1024
        ),
    )(
        orbitals.reshape(NL * NZ, NR, NX),
        potentials.reshape(NPOT * NZ, NR, NX),
        local_potential,
        shifts,
        jnp.asarray(lz),
        jnp.asarray(sx),
        jnp.asarray(sy),
    )
    return out.reshape(NPOT, KZ, KX, NY)


def solution(mesh):
    placed = (
        P("band", None, "gy", None),
        P(None, None, "gy", None),
        P(None, "gy", None),
        P("band"),
    )
    return jax.shard_map(
        per_device,
        mesh=mesh,
        in_specs=placed,
        out_specs=P(None, "band", "gy", None),
        check_vma=False,
    )
```

```python
import jax
import jax.numpy as jnp
import numpy as np
from jax import lax
from jax.experimental import pallas as pl
from jax.experimental.pallas import tpu as pltpu
from jax.sharding import PartitionSpec as P

NX, NY, NZ, NPOT, SWEEPS, NORB = 256, 512, 32, 2, 3, 32
NB, NG = 8, 32
NL = NORB // NB
NR = NY // NG
NF = NL * NPOT
H = 3
KZ, KX = NZ // NB, NX // NG
PK = NPOT * KZ
T = 128
ZO = 8
ROWS = NR + 2 * H
ZB = ZO + NZ
SLAB = ROWS * 2 * ZB + ZO
PIECES = ((3, 3), (6, 3), (9, 4), (13, 3), (0, 3))
FAR_FIRST = sorted(range(1, NG), key=lambda d: -(min(d // 8, 4 - d // 8) + min(d % 8 // 2, 4 - d % 8 // 2)))
GROUP = 4
SPREAD, SCREEN = 3.5, 0.25
MESH = pl.DeviceIdType.MESH
f32, bf16 = jnp.float32, jnp.bfloat16


def sine(length):
    k = np.arange(1, length + 1, dtype=np.float64)
    return np.sqrt(2.0 / (length + 1)) * np.sin(np.pi * np.outer(k, k) / (length + 1))


def halves(table):
    high = table.astype(np.float32).astype(bf16)
    low = (table - high.astype(np.float64)).astype(np.float32).astype(bf16)
    return high, low


def tables():
    zh, zl = halves(sine(NZ))
    lz = np.zeros((NB, NPOT, KZ, NPOT, 3, NZ), bf16)
    for p in range(NPOT):
        for i, part in enumerate((zh, zh, zl)):
            lz[:, p, :, p, i, :] = part.reshape(NB, KZ, NZ)
    lz = lz.reshape(NB * PK, NPOT * 3 * NZ)
    sx = np.stack(halves(sine(NX)))
    sy = np.stack(halves(sine(NY)))
    st, y, j = np.meshgrid(np.arange(NG // 8), np.arange(NR), np.arange(8), indexing="ij")
    sy = sy[:, (NR * (8 * st + j) + y).reshape(-1), :]
    return lz, sx, sy


def split(value):
    high = value.astype(bf16)
    return high, (value - high.astype(f32)).astype(bf16)


def polynomial(shift):
    c = shift + SPREAD
    ratio = c / SPREAD
    now = 1.0 / ratio
    d, r, x = [1.0 / c], [jnp.ones_like(c)], []

    def add(a, b):
        out = []
        for i in range(max(len(a), len(b))):
            if i < len(a) and i < len(b):
                out.append(a[i] + b[i])
            else:
                out.append(a[i] if i < len(a) else b[i])
        return out

    for _ in range(SWEEPS):
        x = add(x, d)
        ad = [c * d[0]]
        for i in range(1, len(d)):
            ad.append(c * d[i] - 0.5 * d[i - 1])
        ad.append(-0.5 * d[-1])
        r = add(r, [-v for v in ad])
        after = 1.0 / (2.0 * ratio - now)
        d = add([after * now * v for v in d], [(2.0 * after / SPREAD) * v for v in r])
        now = after
    return add(x, d)


def kernel(
    orb_hbm, pot_hbm, loc_hbm, shift_ref, lz_hbm, sx_hbm, sy_hbm, out_ref,
    orbv, potv, locv, lz, sx, sy, f0, f1, f2, cf, pc, msg, rmsg,
    e0, e1, part, inbox, dv, ov, rv, wgt,
    load_sem, table_sem, hsend, hrecv, msend, mrecv, rsend, rrecv, asend, arecv,
):
    band, gy = lax.axis_index("band"), lax.axis_index("gy")

    arrays = ((orb_hbm, orbv), (pot_hbm, potv), (loc_hbm, locv))

    def load(low, high):
        for y in range(low, high):
            for i, (src, dst) in enumerate(arrays):
                pltpu.make_async_copy(src.at[:, y], dst.at[H + y], load_sem.at[i, y // GROUP]).start()

    load(0, GROUP)
    barrier = pltpu.get_barrier_semaphore()
    for d in FAR_FIRST:
        pl.semaphore_signal(barrier, 1, device_id=(band, lax.rem(gy + d, NG)), device_id_type=MESH)
    for d in range(1, NB):
        pl.semaphore_signal(barrier, 1, device_id=(lax.rem(band + d, NB), gy), device_id_type=MESH)

    load(GROUP, NR)
    tables_in = []
    for i, (src, dst) in enumerate(((lz_hbm, lz), (sx_hbm, sx), (sy_hbm, sy))):
        tables_in.append(pltpu.make_async_copy(src, dst, table_sem.at[i]))
        tables_in[-1].start()

    zero = jnp.zeros((8, T), f32)

    def clear(i, carry):
        for f in range(NF):
            for field in (f0, f1, f2):
                field[f, pl.ds(pl.multiple_of(i * ZB, 8), ZO), :] = zero
        for n in range(NL):
            e0[n, pl.ds(pl.multiple_of(i * ZB, 8), ZO), :] = zero
        return carry

    lax.fori_loop(0, 2 * ROWS + 1, clear, 0)

    for n in range(NL):
        a = polynomial(jnp.full((8, T), shift_ref[n], f32))
        inverse = 1.0 / a[3]
        pc[n, 0] = a[2] * inverse
        pc[n, 1] = a[1] * inverse
        pc[n, 2] = a[0] * inverse
        pc[n, 3] = -4.0 * a[3]

    def index_of(shape, axis):
        return lax.broadcasted_iota(jnp.int32, shape, axis)

    shape = (PK * KX, NY)
    r_index = index_of(shape, 0)
    kz = band * KZ + lax.rem(lax.div(r_index, KX), KZ)
    kx = gy * KX + lax.rem(r_index, KX)
    qz = jnp.pi * (kz.astype(f32) + 1.0) / (NZ + 1)
    qx = jnp.pi * (kx.astype(f32) + 1.0) / (NX + 1)
    qy = jnp.pi * (index_of(shape, 1).astype(f32) + 1.0) / (NY + 1)
    wgt[...] = jnp.sqrt(4.0 * jnp.pi / (qz * qz + qx * qx + qy * qy + SCREEN))

    def sums(r, acc):
        acc = list(acc)
        for z in range(NZ // 8):
            for x in range(2):
                cols = slice(T * x, T * (x + 1))
                pots = [potv[r, p * NZ + z * 8 : p * NZ + z * 8 + 8, cols] for p in range(NPOT)]
                for n in range(NL):
                    o = orbv[r, n * NZ + z * 8 : n * NZ + z * 8 + 8, cols]
                    q = o * o
                    for p in range(NPOT):
                        acc[p * NL + n] = acc[p * NL + n] + pots[p] * q
                    acc[NF + n] = acc[NF + n] + q
        return tuple(acc)

    acc = tuple(zero for _ in range(NF + NL))
    for g in range(NR // GROUP):
        rows = pl.ds(H + g * GROUP, GROUP)
        for i, (_, dst) in enumerate(arrays):
            pltpu.make_async_copy(dst.at[rows], dst.at[rows], load_sem.at[i, g]).wait()
        acc = lax.fori_loop(H + g * GROUP, H + (g + 1) * GROUP, sums, acc)
    lane1 = lax.broadcasted_iota(jnp.int32, (1, T), 1)
    row = jnp.zeros((1, T), f32)
    for i, a in enumerate(acc):
        total = jnp.sum(jnp.sum(a, axis=0, keepdims=True), axis=1, keepdims=True)
        row = jnp.where(lane1 == i, total, row)
    msg[...] = row

    pl.semaphore_wait(barrier, NG - 1 + NB - 1)

    for d in FAR_FIRST:
        pltpu.make_async_remote_copy(
            msg, rmsg.at[d], msend, mrecv,
            device_id=(band, lax.rem(gy + d, NG)), device_id_type=MESH,
        ).start()

    halo = []
    for side in range(2):
        target = lax.rem(gy + (NG - 1 if side == 0 else 1), NG)
        for i, (_, dst) in enumerate(arrays):
            width = H if i < 2 else H - 1
            if side == 0:
                src, to = pl.ds(H, width), pl.ds(H + NR, width)
            else:
                src, to = pl.ds(H + NR - width, width), pl.ds(H - width, width)
            copy = pltpu.make_async_remote_copy(
                dst.at[src], dst.at[to], hsend.at[side, i], hrecv.at[side, i],
                device_id=(band, target), device_id_type=MESH,
            )
            copy.start()
            halo.append(copy)

    def whole(tile):
        return jnp.concatenate([tile] * (NZ // 8), axis=0)

    def at(r, x, shift=0):
        return pl.ds(pl.multiple_of((r * 2 + x) * ZB + ZO, 8) + shift, NZ)

    def half(ref, r, i, x):
        return ref[r, i * NZ : (i + 1) * NZ, x * T : (x + 1) * T]

    def w_of(r, x):
        return 1.0 - 2.0 * half(locv, r, 0, x)

    def source(r, mask=None):
        for x in range(2):
            pots = [half(potv, r, p, x) for p in range(NPOT)]
            for n in range(NL):
                o = half(orbv, r, n, x)
                if mask is not None:
                    o = o * mask
                for p in range(NPOT):
                    f = n * NPOT + p
                    f0[f, at(r, x), :] = (pots[p] - whole(cf[f])) * o

    lane = lax.broadcasted_iota(jnp.int32, (NZ, T), 1)
    first, last = lane == 0, lane == T - 1
    nought = jnp.zeros((NZ, T), f32)

    def near(field, f, r):
        c = [field[f, at(r, x), :] for x in range(2)]
        up = [pltpu.roll(v, 1, 1) for v in c]
        down = [pltpu.roll(v, T - 1, 1) for v in c]
        beside = [
            jnp.where(first, nought, up[0]) + jnp.where(last, down[1], down[0]),
            jnp.where(first, up[0], up[1]) + jnp.where(last, nought, down[1]),
        ]
        found = []
        for x in range(2):
            z = field[f, at(r, x, -1), :] + field[f, at(r, x, 1), :]
            y = field[f, at(r - 1, x), :] + field[f, at(r + 1, x), :]
            found.append(beside[x] + (z + y))
        return c, found

    def sweep_one(r, mask=None):
        w = [w_of(r, x) for x in range(2)]
        for n in range(NL):
            ws = [w[x] + whole(pc[n, 0]) for x in range(2)]
            for p in range(NPOT):
                f = n * NPOT + p
                c, s = near(f0, f, r)
                for x in range(2):
                    value = s[x] + ws[x] * c[x]
                    f1[f, at(r, x), :] = value if mask is None else value * mask

    def products(r):
        for x in range(2):
            pots = [half(potv, r, p, x) for p in range(NPOT)]
            for n in range(NL):
                o = half(orbv, r, n, x)
                e0[n, at(r, x), :] = o
                for p in range(NPOT):
                    f0[n * NPOT + p, at(r, x), :] = pots[p] * o

    def sweep_products(r):
        w = [w_of(r, x) for x in range(2)]
        for n in range(NL):
            ws = [w[x] + whole(pc[n, 0]) for x in range(2)]
            for src, dst, f in ((f0, f1, n * NPOT), (f0, f1, n * NPOT + 1), (e0, e1, n)):
                c, s = near(src, f, r)
                for x in range(2):
                    dst[f, at(r, x), :] = s[x] + ws[x] * c[x]

    def settle_source(r):
        for x in range(2):
            for n in range(NL):
                o = e0[n, at(r, x), :]
                for p in range(NPOT):
                    f = n * NPOT + p
                    f0[f, at(r, x), :] = f0[f, at(r, x), :] - whole(cf[f]) * o

    def settle_first(r):
        for x in range(2):
            for n in range(NL):
                o = e1[n, at(r, x), :]
                for p in range(NPOT):
                    f = n * NPOT + p
                    f1[f, at(r, x), :] = f1[f, at(r, x), :] - whole(cf[f]) * o

    def sweep_two(r, mask=None):
        w = [w_of(r, x) for x in range(2)]
        for n in range(NL):
            beta = whole(pc[n, 1])
            for p in range(NPOT):
                f = n * NPOT + p
                c, s = near(f1, f, r)
                for x in range(2):
                    value = s[x] + w[x] * c[x] + beta * f0[f, at(r, x), :]
                    f2[f, at(r, x), :] = value if mask is None else value * mask

    def last_sweep(r):
        w = [w_of(r, x) for x in range(2)]
        density = [[None, None] for _ in range(NPOT)]
        for n in range(NL):
            beta, gamma = whole(pc[n, 2]), whole(pc[n, 3])
            orbs = [half(orbv, r, n, x) * gamma for x in range(2)]
            for p in range(NPOT):
                f = n * NPOT + p
                c, s = near(f2, f, r)
                for x in range(2):
                    value = s[x] + w[x] * c[x] + beta * f0[f, at(r, x), :]
                    term = orbs[x] * value
                    old = density[p][x]
                    density[p][x] = term if old is None else old + term
        for x in range(2):
            stack = []
            for p in range(NPOT):
                high, low = split(density[p][x])
                stack += [high, low, high]
            along_z = jnp.dot(lz[...], jnp.concatenate(stack, axis=0), preferred_element_type=f32)
            for b in range(NB):
                part[b, r - H, :, T * x : T * (x + 1)] = along_z[b * PK : (b + 1) * PK, :]

    def send(k, way, kind):
        low, count = PIECES[k]
        far, reach = ((4, 2), (3, 1), (1, 1), (2, 2))[kind]
        rows = part_rows(k, way) if kind == 0 else pl.ds(low, count)
        chunk = lax.rem(band + (far if way == 0 else NB - far), NB)
        to = lax.rem(band + (reach if way == 0 else NB - reach), NB)
        return pltpu.make_async_remote_copy(
            part.at[chunk, rows], inbox.at[way, kind, rows], rsend.at[way, kind, k], rrecv.at[way, kind, k],
            device_id=(to, gy), device_id_type=MESH,
        )

    def part_rows(k, way):
        low, count = PIECES[k]
        cut = (count + (k % 2)) // 2
        return pl.ds(low, cut) if way == 0 else pl.ds(low + cut, count - cut)

    def begin(k):
        for kind in (0, 1, 2):
            for way in range(2):
                send(k, way, kind).start()

    def middle(k):
        low, count = PIECES[k]
        rows = pl.ds(low, count)
        for way in range(2):
            send(k, way, 0).wait_recv()
            send(k, way, 1).wait_recv()
            chunk = lax.rem(band + (2 if way == 0 else NB - 2), NB)
            part[chunk, rows] = part[chunk, rows] + inbox[way, 1, rows]
            some = part_rows(k, way)
            part[chunk, some] = part[chunk, some] + inbox[way, 0, some]
            send(k, way, 3).start()

    def finish(k):
        low, count = PIECES[k]
        rows = pl.ds(low, count)
        for kind in (2, 3):
            for way in range(2):
                send(k, way, kind).wait_recv()
        value = part[band, rows] + ((inbox[0, 2, rows] + inbox[1, 2, rows]) + (inbox[0, 3, rows] + inbox[1, 3, rows]))
        dv[low * PK : (low + count) * PK, :] = value.reshape(count * PK, NX)

    def loop(low, high, body):
        def step(r, carry):
            body(r)
            return carry

        if high == low + 1:
            body(low)
        else:
            lax.fori_loop(low, high, step, 0)

    loop(H, H + NR, products)
    loop(H + 1, H + NR - 1, sweep_products)

    pltpu.make_async_copy(rmsg.at[pl.ds(0, NG - 1)], rmsg.at[pl.ds(0, NG - 1)], mrecv).wait()
    total = msg[...]
    for d in range(1, NG):
        total = total + rmsg[d]
    for n in range(NL):
        norm = total[:, NF + n : NF + n + 1]
        for p in range(NPOT):
            value = total[:, p * NL + n : p * NL + n + 1] / norm
            cf[n * NPOT + p] = jnp.broadcast_to(value, (8, T))

    done = [H, H + 1, H + 2, H + 3]
    for k in range(3):
        end = H + PIECES[k][0] + PIECES[k][1]
        for i, body in enumerate((settle_source, settle_first, sweep_two, last_sweep)):
            stop = min(end + 3 - i, H + NR - i)
            loop(done[i], stop, body)
            done[i] = stop
            if k == 0 and i == 2:
                tables_in[0].wait()
            if k == 2 and i == 2:
                middle(0)
        begin(k)

    low_mask = jnp.where(gy == 0, 0.0, 1.0).astype(f32)
    high_mask = jnp.where(gy == NG - 1, 0.0, 1.0).astype(f32)
    for copy in halo:
        copy.wait_recv()
    top = H + NR
    loop(top, top + 3, lambda r: source(r, high_mask))
    loop(top - 1, top, sweep_one)
    loop(top, top + 2, lambda r: sweep_one(r, high_mask))
    loop(top - 2, top, sweep_two)
    loop(top, top + 1, lambda r: sweep_two(r, high_mask))
    middle(1)
    loop(top - 3, top, last_sweep)
    begin(3)
    loop(0, H, lambda r: source(r, low_mask))
    loop(1, H, lambda r: sweep_one(r, low_mask))
    loop(H, H + 1, sweep_one)
    loop(H - 1, H, lambda r: sweep_two(r, low_mask))
    loop(H, H + 2, sweep_two)
    middle(2)
    loop(H, H + 3, last_sweep)
    begin(4)
    middle(3)
    finish(0)
    finish(1)
    middle(4)
    finish(2)
    finish(3)
    finish(4)

    tables_in[1].wait()
    high, low = split(dv[...])

    def by_rows(a, b):
        return lax.dot_general(a, b, (((1,), (1,)), ((), ())), preferred_element_type=f32)

    along_x = by_rows(sx[0], high) + by_rows(sx[0], low) + by_rows(sx[1], high)
    ov[...] = along_x.reshape(NG, KX, NR * PK)

    for d in FAR_FIRST:
        target = lax.rem(gy + d, NG)
        pltpu.make_async_remote_copy(
            ov.at[target], rv.at[gy], asend, arecv, device_id=(band, target), device_id_type=MESH
        ).start()
    rv[gy] = ov[gy]
    tables_in[2].wait()

    others = pl.ds(0, NG - 1)
    for copy in halo:
        copy.wait_send()
    pltpu.make_async_copy(rmsg.at[pl.ds(0, NG - 1)], rmsg.at[pl.ds(0, NG - 1)], msend).wait()
    for k in range(len(PIECES)):
        for kind in range(4):
            for way in range(2):
                send(k, way, kind).wait_send()
    pltpu.make_async_copy(rv.at[others], rv.at[others], arecv).wait()

    lane8 = lax.rem(lax.broadcasted_iota(jnp.int32, (KX, T), 1), 8)
    along_y = None
    for pair in range(NG // 16):
        columns = []
        for st in (2 * pair, 2 * pair + 1):
            tiles = [rv[st * 8 + j] for j in range(8)]
            column = []
            for pk in range(PK):
                got = None
                for j in range(8):
                    shift = (j - pk) % T
                    moved = tiles[j] if shift == 0 else pltpu.roll(tiles[j], shift, 1)
                    got = moved if got is None else jnp.where(lane8 == j, moved, got)
                column.append(got)
            columns.append(jnp.concatenate(column, axis=0))
        high, low = split(jnp.concatenate(columns, axis=1))
        k_rows = slice(pair * 2 * T, (pair + 1) * 2 * T)
        term = (
            jnp.dot(high, sy[0, k_rows], preferred_element_type=f32)
            + jnp.dot(low, sy[0, k_rows], preferred_element_type=f32)
            + jnp.dot(high, sy[1, k_rows], preferred_element_type=f32)
        )
        along_y = term if along_y is None else along_y + term
    out_ref[...] = along_y * wgt[...]

    pltpu.make_async_copy(rv.at[others], rv.at[others], asend).wait()


def per_device(orbitals, potentials, local_potential, shifts):
    lz, sx, sy = tables()
    anywhere = pl.BlockSpec(memory_space=pl.ANY)
    field = pltpu.VMEM((NF, SLAB, T), f32)
    dma = pltpu.SemaphoreType.DMA
    out = pl.pallas_call(
        kernel,
        out_shape=jax.ShapeDtypeStruct((PK * KX, NY), f32),
        in_specs=[anywhere, anywhere, anywhere, pl.BlockSpec(memory_space=pltpu.SMEM)] + [anywhere] * 3,
        out_specs=pl.BlockSpec(memory_space=pltpu.VMEM),
        scratch_shapes=[
            pltpu.VMEM((ROWS, NL * NZ, NX), f32),
            pltpu.VMEM((ROWS, NPOT * NZ, NX), f32),
            pltpu.VMEM((ROWS, NZ, NX), f32),
            pltpu.VMEM((NB * PK, NPOT * 3 * NZ), bf16),
            pltpu.VMEM((2, NX, NX), bf16),
            pltpu.VMEM((2, NY, NY), bf16),
            field,
            field,
            field,
            pltpu.VMEM((NF, 8, T), f32),
            pltpu.VMEM((NL, 4, 8, T), f32),
            pltpu.VMEM((1, T), f32),
            pltpu.VMEM((NG, 1, T), f32),
            pltpu.VMEM((NL, SLAB, T), f32),
            pltpu.VMEM((NL, SLAB, T), f32),
            pltpu.VMEM((NB, NR, PK, NX), f32),
            pltpu.VMEM((2, 4, NR, PK, NX), f32),
            pltpu.VMEM((NR * PK, NX), f32),
            pltpu.VMEM((NG, KX, NR * PK), f32),
            pltpu.VMEM((NG, KX, NR * PK), f32),
            pltpu.VMEM((PK * KX, NY), f32),
            dma((3, NR // GROUP)),
            dma((3,)),
            dma((2, 3)),
            dma((2, 3)),
            dma,
            dma,
            dma((2, 4, len(PIECES))),
            dma((2, 4, len(PIECES))),
            dma,
            dma,
        ],
        compiler_params=pltpu.CompilerParams(
            collective_id=0, has_side_effects=True, vmem_limit_bytes=56 * 1024 * 1024
        ),
    )(
        orbitals.reshape(NL * NZ, NR, NX),
        potentials.reshape(NPOT * NZ, NR, NX),
        local_potential,
        shifts,
        jnp.asarray(lz),
        jnp.asarray(sx),
        jnp.asarray(sy),
    )
    return out.reshape(NPOT, KZ, KX, NY)


def solution(mesh):
    placed = (
        P("band", None, "gy", None),
        P(None, None, "gy", None),
        P(None, "gy", None),
        P("band"),
    )
    return jax.shard_map(
        per_device,
        mesh=mesh,
        in_specs=placed,
        out_specs=P(None, "band", "gy", None),
        check_vma=False,
    )
```

```python
import jax
import jax.numpy as jnp
import numpy as np
from jax import lax
from jax.experimental import pallas as pl
from jax.experimental.pallas import tpu as pltpu
from jax.sharding import PartitionSpec as P

NX, NY, NZ, NPOT, SWEEPS, NORB = 256, 512, 32, 2, 3, 32
NB, NG = 8, 32
NL = NORB // NB
NR = NY // NG
NF = NL * NPOT
H = 3
KZ, KX = NZ // NB, NX // NG
PK = NPOT * KZ
T = 128
ZO = 8
ROWS = NR + 2 * H
ZB = ZO + NZ
SLAB = ROWS * 2 * ZB + ZO
PIECES = ((3, 2), (5, 3), (8, 5), (13, 3), (0, 3))
FAR_FIRST = sorted(range(1, NG), key=lambda d: -(min(d // 8, 4 - d // 8) + min(d % 8 // 2, 4 - d % 8 // 2)))
GROUP = 4
SPREAD, SCREEN = 3.5, 0.25
MESH = pl.DeviceIdType.MESH
f32, bf16 = jnp.float32, jnp.bfloat16


def sine(length):
    k = np.arange(1, length + 1, dtype=np.float64)
    return np.sqrt(2.0 / (length + 1)) * np.sin(np.pi * np.outer(k, k) / (length + 1))


def halves(table):
    high = table.astype(np.float32).astype(bf16)
    low = (table - high.astype(np.float64)).astype(np.float32).astype(bf16)
    return high, low


def tables():
    zh, zl = halves(sine(NZ))
    lz = np.zeros((NB, NPOT, KZ, NPOT, 3, NZ), bf16)
    for p in range(NPOT):
        for i, part in enumerate((zh, zh, zl)):
            lz[:, p, :, p, i, :] = part.reshape(NB, KZ, NZ)
    lz = lz.reshape(NB * PK, NPOT * 3 * NZ)
    sx = np.stack(halves(sine(NX)))
    sy = np.stack(halves(sine(NY)))
    st, y, j = np.meshgrid(np.arange(NG // 8), np.arange(NR), np.arange(8), indexing="ij")
    sy = sy[:, (NR * (8 * st + j) + y).reshape(-1), :]
    return lz, sx, sy


def split(value):
    high = value.astype(bf16)
    return high, (value - high.astype(f32)).astype(bf16)


def polynomial(shift):
    c = shift + SPREAD
    ratio = c / SPREAD
    now = 1.0 / ratio
    d, r, x = [1.0 / c], [jnp.ones_like(c)], []

    def add(a, b):
        out = []
        for i in range(max(len(a), len(b))):
            if i < len(a) and i < len(b):
                out.append(a[i] + b[i])
            else:
                out.append(a[i] if i < len(a) else b[i])
        return out

    for _ in range(SWEEPS):
        x = add(x, d)
        ad = [c * d[0]]
        for i in range(1, len(d)):
            ad.append(c * d[i] - 0.5 * d[i - 1])
        ad.append(-0.5 * d[-1])
        r = add(r, [-v for v in ad])
        after = 1.0 / (2.0 * ratio - now)
        d = add([after * now * v for v in d], [(2.0 * after / SPREAD) * v for v in r])
        now = after
    return add(x, d)


def kernel(
    orb_hbm, pot_hbm, loc_hbm, shift_ref, lz_hbm, sx_hbm, sy_hbm, out_ref,
    orbv, potv, locv, lz, sx, sy, f0, f1, f2, cf, pc, msg, rmsg,
    e0, e1, part, inbox, dv, ov, rv, wgt,
    load_sem, table_sem, hsend, hrecv, msend, mrecv, rsend, rrecv, asend, arecv,
):
    band, gy = lax.axis_index("band"), lax.axis_index("gy")

    arrays = ((orb_hbm, orbv), (pot_hbm, potv), (loc_hbm, locv))

    def load(low, high):
        for y in range(low, high):
            for i, (src, dst) in enumerate(arrays):
                pltpu.make_async_copy(src.at[:, y], dst.at[H + y], load_sem.at[i, y // GROUP]).start()

    load(0, GROUP)
    barrier = pltpu.get_barrier_semaphore()
    for d in FAR_FIRST:
        pl.semaphore_signal(barrier, 1, device_id=(band, lax.rem(gy + d, NG)), device_id_type=MESH)
    for d in range(1, NB):
        pl.semaphore_signal(barrier, 1, device_id=(lax.rem(band + d, NB), gy), device_id_type=MESH)

    load(GROUP, NR)
    tables_in = []
    for i, (src, dst) in enumerate(((lz_hbm, lz), (sx_hbm, sx), (sy_hbm, sy))):
        tables_in.append(pltpu.make_async_copy(src, dst, table_sem.at[i]))
        tables_in[-1].start()

    zero = jnp.zeros((8, T), f32)

    def clear(i, carry):
        for f in range(NF):
            for field in (f0, f1, f2):
                field[f, pl.ds(pl.multiple_of(i * ZB, 8), ZO), :] = zero
        for n in range(NL):
            e0[n, pl.ds(pl.multiple_of(i * ZB, 8), ZO), :] = zero
        return carry

    lax.fori_loop(0, 2 * ROWS + 1, clear, 0)

    for n in range(NL):
        a = polynomial(jnp.full((8, T), shift_ref[n], f32))
        inverse = 1.0 / a[3]
        pc[n, 0] = a[2] * inverse
        pc[n, 1] = a[1] * inverse
        pc[n, 2] = a[0] * inverse
        pc[n, 3] = -4.0 * a[3]

    def index_of(shape, axis):
        return lax.broadcasted_iota(jnp.int32, shape, axis)

    shape = (PK * KX, NY)
    r_index = index_of(shape, 0)
    kz = band * KZ + lax.rem(lax.div(r_index, KX), KZ)
    kx = gy * KX + lax.rem(r_index, KX)
    qz = jnp.pi * (kz.astype(f32) + 1.0) / (NZ + 1)
    qx = jnp.pi * (kx.astype(f32) + 1.0) / (NX + 1)
    qy = jnp.pi * (index_of(shape, 1).astype(f32) + 1.0) / (NY + 1)
    wgt[...] = jnp.sqrt(4.0 * jnp.pi / (qz * qz + qx * qx + qy * qy + SCREEN))

    def sums(r, acc):
        acc = list(acc)
        for z in range(NZ // 8):
            for x in range(2):
                cols = slice(T * x, T * (x + 1))
                pots = [potv[r, p * NZ + z * 8 : p * NZ + z * 8 + 8, cols] for p in range(NPOT)]
                for n in range(NL):
                    o = orbv[r, n * NZ + z * 8 : n * NZ + z * 8 + 8, cols]
                    q = o * o
                    for p in range(NPOT):
                        acc[p * NL + n] = acc[p * NL + n] + pots[p] * q
                    acc[NF + n] = acc[NF + n] + q
        return tuple(acc)

    acc = tuple(zero for _ in range(NF + NL))
    for g in range(NR // GROUP):
        rows = pl.ds(H + g * GROUP, GROUP)
        for i, (_, dst) in enumerate(arrays):
            pltpu.make_async_copy(dst.at[rows], dst.at[rows], load_sem.at[i, g]).wait()
        acc = lax.fori_loop(H + g * GROUP, H + (g + 1) * GROUP, sums, acc)
    lane1 = lax.broadcasted_iota(jnp.int32, (1, T), 1)
    row = jnp.zeros((1, T), f32)
    for i, a in enumerate(acc):
        total = jnp.sum(jnp.sum(a, axis=0, keepdims=True), axis=1, keepdims=True)
        row = jnp.where(lane1 == i, total, row)
    msg[...] = row

    pl.semaphore_wait(barrier, NG - 1 + NB - 1)

    for d in FAR_FIRST:
        pltpu.make_async_remote_copy(
            msg, rmsg.at[d], msend, mrecv,
            device_id=(band, lax.rem(gy + d, NG)), device_id_type=MESH,
        ).start()

    halo = []
    for side in range(2):
        target = lax.rem(gy + (NG - 1 if side == 0 else 1), NG)
        for i, (_, dst) in enumerate(arrays):
            width = H if i < 2 else H - 1
            if side == 0:
                src, to = pl.ds(H, width), pl.ds(H + NR, width)
            else:
                src, to = pl.ds(H + NR - width, width), pl.ds(H - width, width)
            copy = pltpu.make_async_remote_copy(
                dst.at[src], dst.at[to], hsend.at[side, i], hrecv.at[side, i],
                device_id=(band, target), device_id_type=MESH,
            )
            copy.start()
            halo.append(copy)

    def whole(tile):
        return jnp.concatenate([tile] * (NZ // 8), axis=0)

    def at(r, x, shift=0):
        return pl.ds(pl.multiple_of((r * 2 + x) * ZB + ZO, 8) + shift, NZ)

    def half(ref, r, i, x):
        return ref[r, i * NZ : (i + 1) * NZ, x * T : (x + 1) * T]

    def w_of(r, x):
        return 1.0 - 2.0 * half(locv, r, 0, x)

    def source(r, mask=None):
        for x in range(2):
            pots = [half(potv, r, p, x) for p in range(NPOT)]
            for n in range(NL):
                o = half(orbv, r, n, x)
                if mask is not None:
                    o = o * mask
                for p in range(NPOT):
                    f = n * NPOT + p
                    f0[f, at(r, x), :] = (pots[p] - whole(cf[f])) * o

    lane = lax.broadcasted_iota(jnp.int32, (NZ, T), 1)
    first, last = lane == 0, lane == T - 1
    nought = jnp.zeros((NZ, T), f32)

    def near(field, f, r):
        c = [field[f, at(r, x), :] for x in range(2)]
        up = [pltpu.roll(v, 1, 1) for v in c]
        down = [pltpu.roll(v, T - 1, 1) for v in c]
        beside = [
            jnp.where(first, nought, up[0]) + jnp.where(last, down[1], down[0]),
            jnp.where(first, up[0], up[1]) + jnp.where(last, nought, down[1]),
        ]
        found = []
        for x in range(2):
            z = field[f, at(r, x, -1), :] + field[f, at(r, x, 1), :]
            y = field[f, at(r - 1, x), :] + field[f, at(r + 1, x), :]
            found.append(beside[x] + (z + y))
        return c, found

    def sweep_one(r, mask=None):
        w = [w_of(r, x) for x in range(2)]
        for n in range(NL):
            ws = [w[x] + whole(pc[n, 0]) for x in range(2)]
            for p in range(NPOT):
                f = n * NPOT + p
                c, s = near(f0, f, r)
                for x in range(2):
                    value = s[x] + ws[x] * c[x]
                    f1[f, at(r, x), :] = value if mask is None else value * mask

    def products(r):
        for x in range(2):
            pots = [half(potv, r, p, x) for p in range(NPOT)]
            for n in range(NL):
                o = half(orbv, r, n, x)
                e0[n, at(r, x), :] = o
                for p in range(NPOT):
                    f0[n * NPOT + p, at(r, x), :] = pots[p] * o

    def sweep_products(r):
        w = [w_of(r, x) for x in range(2)]
        for n in range(NL):
            ws = [w[x] + whole(pc[n, 0]) for x in range(2)]
            for src, dst, f in ((f0, f1, n * NPOT), (f0, f1, n * NPOT + 1), (e0, e1, n)):
                c, s = near(src, f, r)
                for x in range(2):
                    dst[f, at(r, x), :] = s[x] + ws[x] * c[x]

    def settle_source(r):
        for x in range(2):
            for n in range(NL):
                o = e0[n, at(r, x), :]
                for p in range(NPOT):
                    f = n * NPOT + p
                    f0[f, at(r, x), :] = f0[f, at(r, x), :] - whole(cf[f]) * o

    def settle_first(r):
        for x in range(2):
            for n in range(NL):
                o = e1[n, at(r, x), :]
                for p in range(NPOT):
                    f = n * NPOT + p
                    f1[f, at(r, x), :] = f1[f, at(r, x), :] - whole(cf[f]) * o

    def sweep_two(r, mask=None):
        w = [w_of(r, x) for x in range(2)]
        for n in range(NL):
            beta = whole(pc[n, 1])
            for p in range(NPOT):
                f = n * NPOT + p
                c, s = near(f1, f, r)
                for x in range(2):
                    value = s[x] + w[x] * c[x] + beta * f0[f, at(r, x), :]
                    f2[f, at(r, x), :] = value if mask is None else value * mask

    def last_sweep(r):
        w = [w_of(r, x) for x in range(2)]
        density = [[None, None] for _ in range(NPOT)]
        for n in range(NL):
            beta, gamma = whole(pc[n, 2]), whole(pc[n, 3])
            orbs = [half(orbv, r, n, x) * gamma for x in range(2)]
            for p in range(NPOT):
                f = n * NPOT + p
                c, s = near(f2, f, r)
                for x in range(2):
                    value = s[x] + w[x] * c[x] + beta * f0[f, at(r, x), :]
                    term = orbs[x] * value
                    old = density[p][x]
                    density[p][x] = term if old is None else old + term
        for x in range(2):
            stack = []
            for p in range(NPOT):
                high, low = split(density[p][x])
                stack += [high, low, high]
            along_z = jnp.dot(lz[...], jnp.concatenate(stack, axis=0), preferred_element_type=f32)
            for b in range(NB):
                part[b, r - H, :, T * x : T * (x + 1)] = along_z[b * PK : (b + 1) * PK, :]

    def send(k, way, kind):
        low, count = PIECES[k]
        far, reach = ((4, 2), (3, 1), (1, 1), (2, 2))[kind]
        rows = part_rows(k, way) if kind == 0 else pl.ds(low, count)
        chunk = lax.rem(band + (far if way == 0 else NB - far), NB)
        to = lax.rem(band + (reach if way == 0 else NB - reach), NB)
        return pltpu.make_async_remote_copy(
            part.at[chunk, rows], inbox.at[way, kind, rows], rsend.at[way, kind, k], rrecv.at[way, kind, k],
            device_id=(to, gy), device_id_type=MESH,
        )

    def part_rows(k, way):
        low, count = PIECES[k]
        cut = (count + (k % 2)) // 2
        return pl.ds(low, cut) if way == 0 else pl.ds(low + cut, count - cut)

    def begin(k):
        for kind in (0, 1, 2):
            for way in range(2):
                send(k, way, kind).start()

    def middle(k):
        low, count = PIECES[k]
        rows = pl.ds(low, count)
        for way in range(2):
            send(k, way, 0).wait_recv()
            send(k, way, 1).wait_recv()
            chunk = lax.rem(band + (2 if way == 0 else NB - 2), NB)
            part[chunk, rows] = part[chunk, rows] + inbox[way, 1, rows]
            some = part_rows(k, way)
            part[chunk, some] = part[chunk, some] + inbox[way, 0, some]
            send(k, way, 3).start()

    def finish(k):
        low, count = PIECES[k]
        rows = pl.ds(low, count)
        for kind in (2, 3):
            for way in range(2):
                send(k, way, kind).wait_recv()
        value = part[band, rows] + ((inbox[0, 2, rows] + inbox[1, 2, rows]) + (inbox[0, 3, rows] + inbox[1, 3, rows]))
        dv[low * PK : (low + count) * PK, :] = value.reshape(count * PK, NX)

    def loop(low, high, body):
        def step(r, carry):
            body(r)
            return carry

        if high == low + 1:
            body(low)
        else:
            lax.fori_loop(low, high, step, 0)

    loop(H, H + NR, products)
    loop(H + 1, H + NR - 1, sweep_products)

    pltpu.make_async_copy(rmsg.at[pl.ds(0, NG - 1)], rmsg.at[pl.ds(0, NG - 1)], mrecv).wait()
    total = msg[...]
    for d in range(1, NG):
        total = total + rmsg[d]
    for n in range(NL):
        norm = total[:, NF + n : NF + n + 1]
        for p in range(NPOT):
            value = total[:, p * NL + n : p * NL + n + 1] / norm
            cf[n * NPOT + p] = jnp.broadcast_to(value, (8, T))

    done = [H, H + 1, H + 2, H + 3]
    for k in range(3):
        end = H + PIECES[k][0] + PIECES[k][1]
        for i, body in enumerate((settle_source, settle_first, sweep_two, last_sweep)):
            stop = min(end + 3 - i, H + NR - i)
            loop(done[i], stop, body)
            done[i] = stop
            if k == 0 and i == 2:
                tables_in[0].wait()
            if k == 2 and i == 2:
                middle(0)
        begin(k)

    low_mask = jnp.where(gy == 0, 0.0, 1.0).astype(f32)
    high_mask = jnp.where(gy == NG - 1, 0.0, 1.0).astype(f32)
    for copy in halo:
        copy.wait_recv()
    top = H + NR
    loop(top, top + 3, lambda r: source(r, high_mask))
    loop(top - 1, top, sweep_one)
    loop(top, top + 2, lambda r: sweep_one(r, high_mask))
    loop(top - 2, top, sweep_two)
    loop(top, top + 1, lambda r: sweep_two(r, high_mask))
    middle(1)
    loop(top - 3, top, last_sweep)
    begin(3)
    loop(0, H, lambda r: source(r, low_mask))
    loop(1, H, lambda r: sweep_one(r, low_mask))
    loop(H, H + 1, sweep_one)
    loop(H - 1, H, lambda r: sweep_two(r, low_mask))
    loop(H, H + 2, sweep_two)
    middle(2)
    loop(H, H + 3, last_sweep)
    begin(4)
    middle(3)
    finish(0)
    finish(1)
    middle(4)
    finish(2)
    finish(3)
    finish(4)

    tables_in[1].wait()
    high, low = split(dv[...])

    def by_rows(a, b):
        return lax.dot_general(a, b, (((1,), (1,)), ((), ())), preferred_element_type=f32)

    along_x = by_rows(sx[0], high) + by_rows(sx[0], low) + by_rows(sx[1], high)
    ov[...] = along_x.reshape(NG, KX, NR * PK)

    for d in FAR_FIRST:
        target = lax.rem(gy + d, NG)
        pltpu.make_async_remote_copy(
            ov.at[target], rv.at[gy], asend, arecv, device_id=(band, target), device_id_type=MESH
        ).start()
    rv[gy] = ov[gy]
    tables_in[2].wait()

    others = pl.ds(0, NG - 1)
    for copy in halo:
        copy.wait_send()
    pltpu.make_async_copy(rmsg.at[pl.ds(0, NG - 1)], rmsg.at[pl.ds(0, NG - 1)], msend).wait()
    for k in range(len(PIECES)):
        for kind in range(4):
            for way in range(2):
                send(k, way, kind).wait_send()
    pltpu.make_async_copy(rv.at[others], rv.at[others], arecv).wait()

    lane8 = lax.rem(lax.broadcasted_iota(jnp.int32, (KX, T), 1), 8)
    along_y = None
    for pair in range(NG // 16):
        columns = []
        for st in (2 * pair, 2 * pair + 1):
            tiles = [rv[st * 8 + j] for j in range(8)]
            column = []
            for pk in range(PK):
                got = None
                for j in range(8):
                    shift = (j - pk) % T
                    moved = tiles[j] if shift == 0 else pltpu.roll(tiles[j], shift, 1)
                    got = moved if got is None else jnp.where(lane8 == j, moved, got)
                column.append(got)
            columns.append(jnp.concatenate(column, axis=0))
        high, low = split(jnp.concatenate(columns, axis=1))
        k_rows = slice(pair * 2 * T, (pair + 1) * 2 * T)
        term = (
            jnp.dot(high, sy[0, k_rows], preferred_element_type=f32)
            + jnp.dot(low, sy[0, k_rows], preferred_element_type=f32)
            + jnp.dot(high, sy[1, k_rows], preferred_element_type=f32)
        )
        along_y = term if along_y is None else along_y + term
    out_ref[...] = along_y * wgt[...]

    pltpu.make_async_copy(rv.at[others], rv.at[others], asend).wait()


def per_device(orbitals, potentials, local_potential, shifts):
    lz, sx, sy = tables()
    anywhere = pl.BlockSpec(memory_space=pl.ANY)
    field = pltpu.VMEM((NF, SLAB, T), f32)
    dma = pltpu.SemaphoreType.DMA
    out = pl.pallas_call(
        kernel,
        out_shape=jax.ShapeDtypeStruct((PK * KX, NY), f32),
        in_specs=[anywhere, anywhere, anywhere, pl.BlockSpec(memory_space=pltpu.SMEM)] + [anywhere] * 3,
        out_specs=pl.BlockSpec(memory_space=pltpu.VMEM),
        scratch_shapes=[
            pltpu.VMEM((ROWS, NL * NZ, NX), f32),
            pltpu.VMEM((ROWS, NPOT * NZ, NX), f32),
            pltpu.VMEM((ROWS, NZ, NX), f32),
            pltpu.VMEM((NB * PK, NPOT * 3 * NZ), bf16),
            pltpu.VMEM((2, NX, NX), bf16),
            pltpu.VMEM((2, NY, NY), bf16),
            field,
            field,
            field,
            pltpu.VMEM((NF, 8, T), f32),
            pltpu.VMEM((NL, 4, 8, T), f32),
            pltpu.VMEM((1, T), f32),
            pltpu.VMEM((NG, 1, T), f32),
            pltpu.VMEM((NL, SLAB, T), f32),
            pltpu.VMEM((NL, SLAB, T), f32),
            pltpu.VMEM((NB, NR, PK, NX), f32),
            pltpu.VMEM((2, 4, NR, PK, NX), f32),
            pltpu.VMEM((NR * PK, NX), f32),
            pltpu.VMEM((NG, KX, NR * PK), f32),
            pltpu.VMEM((NG, KX, NR * PK), f32),
            pltpu.VMEM((PK * KX, NY), f32),
            dma((3, NR // GROUP)),
            dma((3,)),
            dma((2, 3)),
            dma((2, 3)),
            dma,
            dma,
            dma((2, 4, len(PIECES))),
            dma((2, 4, len(PIECES))),
            dma,
            dma,
        ],
        compiler_params=pltpu.CompilerParams(
            collective_id=0, has_side_effects=True, vmem_limit_bytes=56 * 1024 * 1024
        ),
    )(
        orbitals.reshape(NL * NZ, NR, NX),
        potentials.reshape(NPOT * NZ, NR, NX),
        local_potential,
        shifts,
        jnp.asarray(lz),
        jnp.asarray(sx),
        jnp.asarray(sy),
    )
    return out.reshape(NPOT, KZ, KX, NY)


def solution(mesh):
    placed = (
        P("band", None, "gy", None),
        P(None, None, "gy", None),
        P(None, "gy", None),
        P("band"),
    )
    return jax.shard_map(
        per_device,
        mesh=mesh,
        in_specs=placed,
        out_specs=P(None, "band", "gy", None),
        check_vma=False,
    )
```
